32 devices in a mesh: groups: 2 (over y), seq: 4 (over z), dp: 4 (over x, core), head: 1.
Axes of the slice: x: 2, y: 2, z: 4, core: 2. Of those that a mesh axis runs over, the one named last changes fastest.
Arguments:
- x_in: bfloat16 [8, 2048, 768], P(('groups', 'dp'), 'seq'), parts along dimension 0, may hold values from -6 to 6
- kernel_weight: bfloat16 [3, 768, 1536], P(None, None, 'head'), may hold values from -0.125 to 0.125
- conv_bias: float32 [1536], P('head'), may hold values from -3 to 3
- norm_gain: float32 [1536], replicated, may hold values from 0.25 to 1.75
- w_query: bfloat16 [1536, 1024], P(None, 'head'), may hold values from -8 to 8
- w_key: bfloat16 [1536, 128], replicated, may hold values from -1 to 1
- w_value: bfloat16 [1536, 192], replicated, may hold values from -0.15625 to 0.15625
- w_out: bfloat16 [1536, 1536], P('head'), may hold values from -0.15625 to 0.15625
- cotangent: bfloat16 [8, 1024, 1536], P(('groups', 'dp'), 'seq'), parts along dimension 0, may hold values from -0.75 to 0.75
Outputs:
- mixed: bfloat16 [8, 1024, 1536], P(('groups', 'dp'), 'seq', 'head'), parts along dimension 0
- grad_out_t: float32 [3072, 1536], P(('groups', 'dp'), 'head'), parts along dimension 0
The draws below stay inside these ranges and needn't reach their ends.
There are 2 independent parts, one for each index of `groups`. The reference program is written for one: setup_inputs(seed, part) draws one part's arguments, and reference() takes and returns one part's arrays. A program takes and returns all parts, laid end to end along the dimension named above; an argument that names none is the same for every part. Nothing has to cross between parts.
All inputs are finite; a program needn't handle non-finite values.
Results may differ from the reference program's by a relative error of at most 0.02.
Values may be sent and summed in bfloat16 or wider, within the bound.
A program may use at most 128 MiB of HBM per device.

```python
import math
import jax
import jax.numpy as jnp
from jax import lax

C_IN = 768
D = 1536
HEADS = 8
KEY = 128
VAL = 192
KERNEL_TAPS = 3
DILATION_STEP = 2
TOKENS = 1024
ROWS = 2048
SAMPLES = 4


def shared_keys(key):
    return jax.random.normal(jax.random.fold_in(key, 11), (D, KEY), jnp.float32) / math.sqrt(D)


def draw_w_key(key, part):
    return shared_keys(key).astype(jnp.bfloat16)


def draw_w_query(key, part):
    perturb = jax.random.normal(jax.random.fold_in(key, 12), (D, HEADS, KEY), jnp.float32) / math.sqrt(D)
    blended = 2.5 * perturb
    blended = jnp.clip(blended, -8.0, 8.0)
    return blended.reshape(D, HEADS * KEY).astype(jnp.bfloat16)


def level_of(own_key, dims, shards, least, top_value):
    def one(axis_at, blocks):
        draws = jax.random.uniform(jax.random.fold_in(jax.random.fold_in(own_key, 6), axis_at), (blocks,), jnp.float32, least / len(shards), top_value / len(shards))
        return jnp.repeat(jnp.exp(draws), dims[axis_at] // blocks).reshape((-1,) + (1,) * (len(dims) - axis_at - 1))

    gain = one(*shards[0])
    for cut in shards[1:]:
        gain = gain * one(*cut)
    return gain


def centred(rng, dims, spread, limit, cuts=(), kind=jnp.bfloat16):
    array = spread * jax.random.normal(rng, dims, jnp.float32)
    if cuts:
        array = array * level_of(rng, dims, cuts, -0.22, 0.18)
    return jnp.clip(array, -limit, limit).astype(kind)


def setup_inputs(seed: int = 0, part: int = 0) -> dict:
    streams_of = jax.random.split(jax.random.key(seed), 10)
    part_keys = jax.random.split(jax.random.fold_in(streams_of[9], part), 10)
    return {
        "x_in": centred(part_keys[0], (SAMPLES, ROWS, C_IN), 1.0, 6.0, ((0, 4), (1, 4))),
        "kernel_weight": centred(streams_of[1], (KERNEL_TAPS, C_IN, D), (KERNEL_TAPS * C_IN) ** -0.5, 0.125),
        "conv_bias": centred(streams_of[2], (D,), 0.5, 3.0, (), jnp.float32),
        "norm_gain": jnp.clip(1.0 + 0.15 * jax.random.normal(streams_of[3], (D,), jnp.float32), 0.25, 1.75),
        "w_query": draw_w_query(jax.random.fold_in(streams_of[9], 71), part),
        "w_key": draw_w_key(jax.random.fold_in(streams_of[9], 71), part),
        "w_value": centred(streams_of[6], (D, VAL), D ** -0.5, 0.15625),
        "w_out": centred(streams_of[7], (HEADS * VAL, D), (HEADS * VAL) ** -0.5, 0.15625),
        "cotangent": centred(part_keys[8], (SAMPLES, TOKENS, D), (3.0 / (SAMPLES * TOKENS) ** 0.5), 0.75, ((0, 4), (1, 4))),
    }


rope_base = 10000.0
norm_eps = 1e-06

def rotate(vectors, positions):
    halfway = vectors.shape[-1] // 2
    frequency = jnp.exp(-math.log(rope_base) * 2.0 * jnp.arange(halfway, dtype=jnp.float32) / vectors.shape[-1])
    angles = positions.astype(jnp.float32)[:, None] * frequency[None, :]
    layout = (positions.shape[0],) + (1,) * (vectors.ndim - 2) + (halfway,)
    cosine = jnp.cos(angles).reshape(layout)
    sines = jnp.sin(angles).reshape(layout)
    leading = vectors[..., :halfway]
    trailing = vectors[..., halfway:]
    return jnp.concatenate([leading * cosine - trailing * sines, leading * sines + trailing * cosine], axis=-1)

def encode_slab(inputs, kernel_weight, conv_bias):
    edge_padding = DILATION_STEP * (KERNEL_TAPS - 1) // 2
    padded_rows = jnp.pad(inputs, ((edge_padding, edge_padding), (0, 0)))
    padded_row_count = inputs.shape[0]
    before_activation = conv_bias[None, :] + jnp.zeros((padded_row_count, kernel_weight.shape[2]), jnp.float32)
    for kernel_tap_index in range(KERNEL_TAPS):
        before_activation = before_activation + jnp.dot(padded_rows[kernel_tap_index * DILATION_STEP:kernel_tap_index * DILATION_STEP + padded_row_count], kernel_weight[kernel_tap_index], preferred_element_type=jnp.float32)
    activated = jax.nn.gelu(before_activation)
    return lax.optimization_barrier(jnp.max(activated.reshape(padded_row_count // 2, 2, -1), axis=1)).astype(jnp.bfloat16)

def reference(x_in, kernel_weight, conv_bias, norm_gain, w_query, w_key, w_value, w_out, cotangent):
    pooled = lax.map(lambda inputs: encode_slab(inputs, kernel_weight, conv_bias), x_in)
    widened = pooled.astype(jnp.float32)
    squares = lax.optimization_barrier(jnp.mean(widened * widened, axis=-1, keepdims=True))
    normed = (widened * lax.rsqrt(squares + norm_eps) * norm_gain).astype(jnp.bfloat16)
    positions = jnp.arange(TOKENS, dtype=jnp.int32)
    block_size = math.gcd(TOKENS, 512)

    def one_sample(normed_rows):
        queries = rotate(jnp.dot(normed_rows, w_query, preferred_element_type=jnp.float32).reshape(TOKENS, HEADS, KEY), positions).astype(jnp.bfloat16)
        key_rows = rotate(jnp.dot(normed_rows, w_key, preferred_element_type=jnp.float32), positions).astype(jnp.bfloat16)
        value_rows = jnp.dot(normed_rows, w_value, preferred_element_type=jnp.float32).astype(jnp.bfloat16)
        key_wide = key_rows.astype(jnp.float32)
        value_wide = value_rows.astype(jnp.float32)

        def one_block(query_block):
            scores = jnp.einsum('thd,ud->htu', query_block.astype(jnp.float32), key_wide) * KEY ** (-0.5)
            peak = lax.optimization_barrier(jnp.max(scores, axis=-1, keepdims=True))
            weights = jnp.exp(scores - peak)
            totals = lax.optimization_barrier(jnp.sum(weights, axis=-1))
            rounded = lax.optimization_barrier(weights.astype(jnp.bfloat16))
            weighted = jnp.einsum('htu,uv->thv', rounded.astype(jnp.float32), value_wide)
            return (weighted / jnp.transpose(totals)[:, :, None]).astype(jnp.bfloat16)
        blocks = queries.reshape(TOKENS // block_size, block_size, HEADS, KEY)
        return lax.map(one_block, blocks).reshape(TOKENS, HEADS * VAL)
    attended = lax.map(one_sample, normed)
    projected = jnp.einsum('btj,jo->bto', attended.astype(jnp.float32), w_out.astype(jnp.float32))
    mixed = (pooled.astype(jnp.float32) + projected).astype(jnp.bfloat16)
    grad_out_t = jnp.einsum('bto,btj->oj', cotangent.astype(jnp.float32), attended.astype(jnp.float32))
    return (mixed, grad_out_t)
```

```python
import functools
import math

import jax
import jax.numpy as jnp
from jax import lax
from jax.experimental import pallas as pl
from jax.experimental.pallas import tpu as pltpu
from jax.sharding import PartitionSpec as P

KEY = 128
VAL = 192
KERNEL_TAPS = 3
DILATION_STEP = 2


rope_base = 10000.0
norm_eps = 1e-06


def padded(cells, sides, width):
    for axis, dim in sides:
        count = lax.axis_size(axis)
        ends = count - 1
        head = lax.slice_in_dim(cells, 0, width, axis=dim)
        tail = lax.slice_in_dim(cells, cells.shape[dim] - width, cells.shape[dim], axis=dim)
        cells = jnp.concatenate(
            [
                lax.ppermute(tail, axis, [(i, (i + 1) % count) for i in range(ends)]),
                cells,
                lax.ppermute(head, axis, [((i + 1) % count, i) for i in range(ends)]),
            ],
            axis=dim,
        )
    return cells


def rotate(vectors, positions):
    halfway = vectors.shape[-1] // 2
    frequency = jnp.exp(
        -math.log(rope_base) * 2.0 * jnp.arange(halfway, dtype=jnp.float32) / vectors.shape[-1]
    )
    angles = positions.astype(jnp.float32)[:, None] * frequency[None, :]
    layout = (positions.shape[0],) + (1,) * (vectors.ndim - 2) + (halfway,)
    cosine = jnp.cos(angles).reshape(layout)
    sines = jnp.sin(angles).reshape(layout)
    leading = vectors[..., :halfway]
    trailing = vectors[..., halfway:]
    return jnp.concatenate(
        [leading * cosine - trailing * sines, leading * sines + trailing * cosine], axis=-1
    )


def attend_pieces(queries, key_rows, value_rows, state_in):
    total_keys = key_rows.shape[0]
    block_size = math.gcd(total_keys, 512)

    def one_block(block_index, state):
        running_max, running_sum, weighted = state
        key_block = lax.dynamic_slice_in_dim(key_rows, block_index * block_size, block_size, 0)
        value_block = lax.dynamic_slice_in_dim(value_rows, block_index * block_size, block_size, 0)
        scores = jnp.einsum(
            "thd,ud->htu", queries, key_block, preferred_element_type=jnp.float32
        ) * KEY ** (-0.5)
        new_max = jnp.maximum(running_max, jnp.max(scores, axis=-1))
        rescale = jnp.exp(running_max - new_max)
        weights = jnp.exp(scores - new_max[:, :, None])
        running_sum = running_sum * rescale + jnp.sum(weights, axis=-1)
        weighted = weighted * jnp.transpose(rescale)[:, :, None] + jnp.einsum(
            "htu,uv->thv",
            weights.astype(jnp.bfloat16),
            value_block,
            preferred_element_type=jnp.float32,
        )
        return (new_max, running_sum, weighted)

    return lax.fori_loop(0, total_keys // block_size, one_block, state_in)


def signal_to(sem, where):
    pl.semaphore_signal(sem, inc=1, device_id=where, device_id_type=pl.DeviceIdType.MESH)


def remote(src, dst, send_sem, recv_sem, where):
    return pltpu.make_async_remote_copy(
        src_ref=src,
        dst_ref=dst,
        send_sem=send_sem,
        recv_sem=recv_sem,
        device_id=where,
        device_id_type=pl.DeviceIdType.MESH,
    )


class Plan:
    def __init__(self, tokens, width, columns, dp, seq):
        self.tokens, self.width, self.columns = tokens, width, columns
        self.dp, self.seq = dp, seq
        self.levels = dp.bit_length() - 1
        self.block = width // dp
        self.rows = 128 if self.block % 128 == 0 else self.block
        self.pieces = self.block // self.rows
        self.chunk = 2 * VAL
        self.chunks = columns // self.chunk
        self.units = self.chunks * self.pieces

    def scratch(self):
        tile = (self.rows, self.chunk)
        shapes = [
            pltpu.VMEM((self.width, self.tokens), jnp.bfloat16),
            pltpu.VMEM((self.chunks, self.tokens, self.chunk), jnp.bfloat16),
            pltpu.VMEM((self.units,) + tile, jnp.float32),
        ]
        sends = self.levels + 2
        for level in range(self.levels):
            held = self.dp >> (level + 1)
            shapes += [pltpu.VMEM((self.units, held) + tile, jnp.bfloat16)] * 2
        shapes += [pltpu.VMEM((self.units,) + tile, jnp.bfloat16)] * 4
        shapes += [pltpu.SemaphoreType.DMA((self.units,))] * (2 * sends)
        return shapes


def gradient_loop(plan, refs, out_ref):
    cot_t, att, own = refs[:3]
    levels, units = plan.levels, plan.units
    pairs = refs[3 : 3 + 2 * levels]
    ahead_out, ahead_in, back_out, back_in = refs[3 + 2 * levels : 7 + 2 * levels]
    sems = refs[7 + 2 * levels :]
    d = lax.axis_index("dp")
    s = lax.axis_index("seq")
    gap = 2
    last = plan.seq - 1

    def product(unit, p):
        start = pl.multiple_of(
            p * plan.block + (unit % plan.pieces) * plan.rows, plan.rows
        )
        return jnp.dot(
            cot_t[pl.ds(start, plan.rows), :],
            att[unit // plan.pieces],
            preferred_element_type=jnp.float32,
        )

    def summed(unit, p, level):
        value = product(unit, p)
        for done in range(level):
            value = value + pairs[2 * done + 1][unit, p // (2 << done)].astype(jnp.float32)
        return value

    def level_copy(unit, level):
        step = 1 << level
        peer = d + (1 - 2 * ((d // step) % 2)) * step
        return remote(
            pairs[2 * level].at[unit],
            pairs[2 * level + 1].at[unit],
            sems[2 * level].at[unit],
            sems[2 * level + 1].at[unit],
            {"dp": peer},
        )

    def ahead_copy(unit):
        at = 2 * levels
        return remote(
            ahead_out.at[unit], ahead_in.at[unit], sems[at].at[unit], sems[at + 1].at[unit],
            {"seq": s + 1},
        )

    def back_copy(unit):
        at = 2 * levels + 2
        return remote(
            back_out.at[unit], back_in.at[unit], sems[at].at[unit], sems[at + 1].at[unit],
            {"seq": s - 1},
        )

    def within(unit):
        return jnp.logical_and(unit >= 0, unit < units)

    def step_at(t, carry):
        for level in range(levels):
            unit = t - gap * level

            @pl.when(within(unit))
            def _(unit=unit, level=level):
                if level > 0:
                    level_copy(unit, level - 1).wait_recv()
                step = 1 << level
                base = d % step + (1 - (d // step) % 2) * step
                for i in range(plan.dp >> (level + 1)):
                    pairs[2 * level][unit, i] = summed(unit, base + i * 2 * step, level).astype(
                        jnp.bfloat16
                    )
                level_copy(unit, level).start()

        unit = t - gap * levels

        @pl.when(within(unit))
        def _():
            if levels > 0:
                level_copy(unit, levels - 1).wait_recv()
            own[unit] = summed(unit, d, levels)

        if last > 0:
            fore = t - gap * (levels + s)

            @pl.when(jnp.logical_and(within(fore), s == 0))
            def _():
                ahead_out[fore] = own[fore].astype(jnp.bfloat16)
                ahead_copy(fore).start()

            @pl.when(jnp.logical_and(within(fore), s > 0))
            def _():
                ahead_copy(fore).wait_recv()

                @pl.when(s < last)
                def _():
                    ahead_out[fore] = (own[fore] + ahead_in[fore].astype(jnp.float32)).astype(
                        jnp.bfloat16
                    )
                    ahead_copy(fore).start()

            rear = t - gap * (levels + last - s)

            @pl.when(jnp.logical_and(within(rear), s == last))
            def _():
                back_out[rear] = own[rear].astype(jnp.bfloat16)
                back_copy(rear).start()

            @pl.when(jnp.logical_and(within(rear), s < last))
            def _():
                back_copy(rear).wait_recv()

                @pl.when(s > 0)
                def _():
                    back_out[rear] = (own[rear] + back_in[rear].astype(jnp.float32)).astype(
                        jnp.bfloat16
                    )
                    back_copy(rear).start()

        ready = t - gap * (levels + last)

        def store(value):
            row = pl.multiple_of((ready % plan.pieces) * plan.rows, plan.rows)
            column = pl.multiple_of((ready // plan.pieces) * plan.chunk, plan.chunk)
            out_ref[pl.ds(row, plan.rows), pl.ds(column, plan.chunk)] = value

        if last == 0:

            @pl.when(within(ready))
            def _():
                store(own[ready])

        else:

            @pl.when(jnp.logical_and(within(ready), s == 0))
            def _():
                store(own[ready] + back_in[ready].astype(jnp.float32))

            @pl.when(jnp.logical_and(within(ready), s == last))
            def _():
                store(own[ready] + ahead_in[ready].astype(jnp.float32))

            if last > 1:

                @pl.when(
                    jnp.logical_and(within(ready), jnp.logical_and(s > 0, s < last))
                )
                def _():
                    store(
                        own[ready]
                        + ahead_in[ready].astype(jnp.float32)
                        + back_in[ready].astype(jnp.float32)
                    )

        return carry

    lax.fori_loop(0, units + gap * (levels + last), step_at, 0)

    def drain(unit, carry):
        for level in range(levels):
            level_copy(unit, level).wait_send()
        if last > 0:

            @pl.when(s < last)
            def _():
                ahead_copy(unit).wait_send()

            @pl.when(s > 0)
            def _():
                back_copy(unit).wait_send()

        return carry

    lax.fori_loop(0, units, drain, 0)


def greet(plan):
    barrier = pltpu.get_barrier_semaphore()
    d = lax.axis_index("dp")
    s = lax.axis_index("seq")
    for level in range(plan.levels):
        step = 1 << level
        signal_to(barrier, {"dp": d + (1 - 2 * ((d // step) % 2)) * step})
    if plan.seq > 1:

        @pl.when(s > 0)
        def _():
            signal_to(barrier, {"seq": s - 1})

        @pl.when(s < plan.seq - 1)
        def _():
            signal_to(barrier, {"seq": s + 1})

    if plan.seq == 1:
        pl.semaphore_wait(barrier, plan.levels)
        return
    edge = jnp.logical_or(s == 0, s == plan.seq - 1)

    @pl.when(edge)
    def _():
        pl.semaphore_wait(barrier, plan.levels + 1)

    @pl.when(jnp.logical_not(edge))
    def _():
        pl.semaphore_wait(barrier, plan.levels + 2)


def gradient_kernel(plan, cot_ref, att_ref, out_ref, *refs):
    greet(plan)
    refs[0][...] = jnp.transpose(cot_ref[...])
    for c in range(plan.chunks):
        refs[1][c] = att_ref[:, c * plan.chunk : (c + 1) * plan.chunk]
    gradient_loop(plan, refs, out_ref)


def reduced_gradient(upstream, attended):
    plan = Plan(
        upstream.shape[0], upstream.shape[1], attended.shape[1],
        lax.axis_size("dp"), lax.axis_size("seq"),
    )
    whole = pl.BlockSpec(memory_space=pltpu.VMEM)
    return pl.pallas_call(
        functools.partial(gradient_kernel, plan),
        out_shape=jax.ShapeDtypeStruct((plan.block, plan.columns), jnp.float32),
        in_specs=[whole, whole],
        out_specs=whole,
        scratch_shapes=plan.scratch(),
        compiler_params=pltpu.CompilerParams(
            collective_id=0, has_side_effects=True, vmem_limit_bytes=56 * 2**20
        ),
        name="reduced_gradient",
    )(upstream, attended)


def local(x_in, kernel_weight, conv_bias, norm_gain, w_query, w_key, w_value, w_out, cotangent):
    inputs = x_in[0]
    edge_padding = DILATION_STEP * (KERNEL_TAPS - 1) // 2
    padded_rows = padded(inputs, (("seq", 0),), edge_padding)
    padded_row_count = inputs.shape[0]
    before_activation = jnp.broadcast_to(
        conv_bias[None, :], (padded_row_count, kernel_weight.shape[2])
    )
    for kernel_tap_index in range(KERNEL_TAPS):
        before_activation = before_activation + jnp.dot(
            padded_rows[
                kernel_tap_index * DILATION_STEP : kernel_tap_index * DILATION_STEP
                + padded_row_count
            ],
            kernel_weight[kernel_tap_index],
            preferred_element_type=jnp.float32,
        )
    activated = jax.nn.gelu(before_activation)
    pooled = jnp.max(activated.reshape(padded_row_count // 2, 2, -1), axis=1).astype(jnp.bfloat16)
    token_count = pooled.shape[0]
    features = lax.all_gather(pooled, "head", axis=1, tiled=True)
    widened = features.astype(jnp.float32)
    squares = jnp.mean(widened * widened, axis=-1, keepdims=True)
    normed = (widened * lax.rsqrt(squares + norm_eps) * norm_gain).astype(jnp.bfloat16)
    seq_offset = lax.axis_index("seq") * token_count
    positions = seq_offset + jnp.arange(token_count, dtype=jnp.int32)
    local_heads = w_query.shape[1] // KEY
    queries = rotate(
        jnp.dot(normed, w_query, preferred_element_type=jnp.float32).reshape(
            token_count, local_heads, KEY
        ),
        positions,
    ).astype(jnp.bfloat16)
    own_rows = token_count // lax.axis_size("head")
    row_offset = lax.axis_index("head") * own_rows
    own_normed = lax.dynamic_slice_in_dim(normed, row_offset, own_rows, 0)
    own_positions = seq_offset + row_offset + jnp.arange(own_rows, dtype=jnp.int32)
    key_rows = rotate(
        jnp.dot(own_normed, w_key, preferred_element_type=jnp.float32), own_positions
    ).astype(jnp.bfloat16)
    value_rows = jnp.dot(own_normed, w_value, preferred_element_type=jnp.float32).astype(
        jnp.bfloat16
    )
    start_state = (
        jnp.full((local_heads, token_count), -1e30, jnp.float32),
        jnp.zeros((local_heads, token_count), jnp.float32),
        jnp.zeros((token_count, local_heads, VAL), jnp.float32),
    )
    both = lax.all_gather(
        jnp.concatenate([key_rows, value_rows], axis=1), ("seq", "head"), axis=0, tiled=True
    )
    final_state = attend_pieces(
        queries,
        both[:, :KEY],
        both[:, KEY:],
        start_state,
    )
    running_max, running_sum, weighted = final_state
    attended = (
        (weighted / jnp.transpose(running_sum)[:, :, None])
        .astype(jnp.bfloat16)
        .reshape(token_count, local_heads * VAL)
    )
    projected = lax.psum_scatter(
        lax.dot_general(
            w_out, attended, (((0,), (1,)), ((), ())), preferred_element_type=jnp.float32
        ).astype(jnp.bfloat16),
        "head",
        scatter_dimension=0,
        tiled=True,
    ).astype(jnp.float32)
    mixed = (pooled.astype(jnp.float32) + jnp.transpose(projected)).astype(jnp.bfloat16)[None]
    upstream = cotangent[0]
    gradient = reduced_gradient(upstream, attended)
    return (mixed, gradient)


def solution(mesh):
    return jax.shard_map(
        local,
        mesh=mesh,
        in_specs=(
            P(("groups", "dp"), "seq", None),
            P(None, None, "head"),
            P("head"),
            P(),
            P(None, "head"),
            P(),
            P(),
            P("head", None),
            P(("groups", "dp"), "seq", None),
        ),
        out_specs=(P(("groups", "dp"), "seq", "head"), P(("groups", "dp"), "head")),
        check_vma=False,
    )
```

```python
import functools
import math

import jax
import jax.numpy as jnp
from jax import lax
from jax.experimental import pallas as pl
from jax.experimental.pallas import tpu as pltpu
import numpy as np
from jax.sharding import PartitionSpec as P

KEY = 128
VAL = 192
KERNEL_TAPS = 3
DILATION_STEP = 2


rope_base = 10000.0
norm_eps = 1e-06


def padded(cells, sides, width):
    for axis, dim in sides:
        count = lax.axis_size(axis)
        ends = count - 1
        head = lax.slice_in_dim(cells, 0, width, axis=dim)
        tail = lax.slice_in_dim(cells, cells.shape[dim] - width, cells.shape[dim], axis=dim)
        cells = jnp.concatenate(
            [
                lax.ppermute(tail, axis, [(i, (i + 1) % count) for i in range(ends)]),
                cells,
                lax.ppermute(head, axis, [((i + 1) % count, i) for i in range(ends)]),
            ],
            axis=dim,
        )
    return cells


def rotate(vectors, positions):
    halfway = vectors.shape[-1] // 2
    frequency = jnp.exp(
        -math.log(rope_base) * 2.0 * jnp.arange(halfway, dtype=jnp.float32) / vectors.shape[-1]
    )
    angles = positions.astype(jnp.float32)[:, None] * frequency[None, :]
    layout = (positions.shape[0],) + (1,) * (vectors.ndim - 2) + (halfway,)
    cosine = jnp.cos(angles).reshape(layout)
    sines = jnp.sin(angles).reshape(layout)
    leading = vectors[..., :halfway]
    trailing = vectors[..., halfway:]
    return jnp.concatenate(
        [leading * cosine - trailing * sines, leading * sines + trailing * cosine], axis=-1
    )


def attend_pieces(queries, key_rows, value_rows, state_in):
    total_keys = key_rows.shape[0]
    block_size = math.gcd(total_keys, 512)

    def one_block(block_index, state):
        running_max, running_sum, weighted = state
        key_block = lax.dynamic_slice_in_dim(key_rows, block_index * block_size, block_size, 0)
        value_block = lax.dynamic_slice_in_dim(value_rows, block_index * block_size, block_size, 0)
        scores = jnp.einsum(
            "thd,ud->htu", queries, key_block, preferred_element_type=jnp.float32
        ) * KEY ** (-0.5)
        new_max = jnp.maximum(running_max, jnp.max(scores, axis=-1))
        rescale = jnp.exp(running_max - new_max)
        weights = jnp.exp(scores - new_max[:, :, None])
        running_sum = running_sum * rescale + jnp.sum(weights, axis=-1)
        weighted = weighted * jnp.transpose(rescale)[:, :, None] + jnp.einsum(
            "htu,uv->thv",
            weights.astype(jnp.bfloat16),
            value_block,
            preferred_element_type=jnp.float32,
        )
        return (new_max, running_sum, weighted)

    return lax.fori_loop(0, total_keys // block_size, one_block, state_in)


def signal_to(sem, where):
    pl.semaphore_signal(sem, inc=1, device_id=where, device_id_type=pl.DeviceIdType.MESH)


def remote(src, dst, send_sem, recv_sem, where):
    return pltpu.make_async_remote_copy(
        src_ref=src,
        dst_ref=dst,
        send_sem=send_sem,
        recv_sem=recv_sem,
        device_id=where,
        device_id_type=pl.DeviceIdType.MESH,
    )


class Plan:
    def __init__(self, tokens, width, columns, dp, seq):
        self.tokens, self.width, self.columns = tokens, width, columns
        self.dp, self.seq = dp, seq
        self.levels = dp.bit_length() - 1
        self.block = width // dp
        self.rows = 128 if self.block % 128 == 0 else self.block
        self.pieces = self.block // self.rows
        self.chunk = 2 * VAL
        self.chunks = columns // self.chunk
        self.units = self.chunks * self.pieces

    def scratch(self):
        tile = (self.rows, self.chunk)
        shapes = [
            pltpu.VMEM((self.width, self.tokens), jnp.bfloat16),
            pltpu.VMEM((self.chunks, self.tokens, self.chunk), jnp.bfloat16),
            pltpu.VMEM((self.units,) + tile, jnp.float32),
        ]
        sends = self.levels + 2
        for level in range(self.levels):
            held = self.dp >> (level + 1)
            shapes += [pltpu.VMEM((self.units, held) + tile, jnp.bfloat16)] * 2
        shapes += [pltpu.VMEM((self.units,) + tile, jnp.bfloat16)] * 4
        shapes += [pltpu.SemaphoreType.DMA((self.units,))] * (2 * sends)
        return shapes


def gradient_loop(plan, refs, out_ref, produce=None, least=0):
    cot_t, att, own = refs[:3]
    levels, units = plan.levels, plan.units
    pairs = refs[3 : 3 + 2 * levels]
    ahead_out, ahead_in, back_out, back_in = refs[3 + 2 * levels : 7 + 2 * levels]
    sems = refs[7 + 2 * levels :]
    d = lax.axis_index("dp")
    s = lax.axis_index("seq")
    gap = 2
    last = plan.seq - 1

    def product(unit, p):
        start = pl.multiple_of(
            p * plan.block + (unit % plan.pieces) * plan.rows, plan.rows
        )
        return jnp.dot(
            cot_t[pl.ds(start, plan.rows), :],
            att[unit // plan.pieces],
            preferred_element_type=jnp.float32,
        )

    def summed(unit, p, level):
        value = product(unit, p)
        for done in range(level):
            value = value + pairs[2 * done + 1][unit, p // (2 << done)].astype(jnp.float32)
        return value

    def level_copy(unit, level):
        step = 1 << level
        peer = d + (1 - 2 * ((d // step) % 2)) * step
        return remote(
            pairs[2 * level].at[unit],
            pairs[2 * level + 1].at[unit],
            sems[2 * level].at[unit],
            sems[2 * level + 1].at[unit],
            {"dp": peer},
        )

    def ahead_copy(unit):
        at = 2 * levels
        return remote(
            ahead_out.at[unit], ahead_in.at[unit], sems[at].at[unit], sems[at + 1].at[unit],
            {"seq": s + 1},
        )

    def back_copy(unit):
        at = 2 * levels + 2
        return remote(
            back_out.at[unit], back_in.at[unit], sems[at].at[unit], sems[at + 1].at[unit],
            {"seq": s - 1},
        )

    def within(unit):
        return jnp.logical_and(unit >= 0, unit < units)

    def step_at(t, carry):
        if produce is not None:
            produce(t)
        for level in range(levels):
            unit = t - gap * level

            @pl.when(within(unit))
            def _(unit=unit, level=level):
                if level > 0:
                    level_copy(unit, level - 1).wait_recv()
                step = 1 << level
                base = d % step + (1 - (d // step) % 2) * step
                for i in range(plan.dp >> (level + 1)):
                    pairs[2 * level][unit, i] = summed(unit, base + i * 2 * step, level).astype(
                        jnp.bfloat16
                    )
                level_copy(unit, level).start()

        unit = t - gap * levels

        @pl.when(within(unit))
        def _():
            if levels > 0:
                level_copy(unit, levels - 1).wait_recv()
            own[unit] = summed(unit, d, levels)

        if last > 0:
            fore = t - gap * (levels + s)

            @pl.when(jnp.logical_and(within(fore), s == 0))
            def _():
                ahead_out[fore] = own[fore].astype(jnp.bfloat16)
                ahead_copy(fore).start()

            @pl.when(jnp.logical_and(within(fore), s > 0))
            def _():
                ahead_copy(fore).wait_recv()

                @pl.when(s < last)
                def _():
                    ahead_out[fore] = (own[fore] + ahead_in[fore].astype(jnp.float32)).astype(
                        jnp.bfloat16
                    )
                    ahead_copy(fore).start()

            rear = t - gap * (levels + last - s)

            @pl.when(jnp.logical_and(within(rear), s == last))
            def _():
                back_out[rear] = own[rear].astype(jnp.bfloat16)
                back_copy(rear).start()

            @pl.when(jnp.logical_and(within(rear), s < last))
            def _():
                back_copy(rear).wait_recv()

                @pl.when(s > 0)
                def _():
                    back_out[rear] = (own[rear] + back_in[rear].astype(jnp.float32)).astype(
                        jnp.bfloat16
                    )
                    back_copy(rear).start()

        ready = t - gap * (levels + last)

        def store(value):
            row = pl.multiple_of((ready % plan.pieces) * plan.rows, plan.rows)
            column = pl.multiple_of((ready // plan.pieces) * plan.chunk, plan.chunk)
            out_ref[pl.ds(row, plan.rows), pl.ds(column, plan.chunk)] = value

        if last == 0:

            @pl.when(within(ready))
            def _():
                store(own[ready])

        else:

            @pl.when(jnp.logical_and(within(ready), s == 0))
            def _():
                store(own[ready] + back_in[ready].astype(jnp.float32))

            @pl.when(jnp.logical_and(within(ready), s == last))
            def _():
                store(own[ready] + ahead_in[ready].astype(jnp.float32))

            if last > 1:

                @pl.when(
                    jnp.logical_and(within(ready), jnp.logical_and(s > 0, s < last))
                )
                def _():
                    store(
                        own[ready]
                        + ahead_in[ready].astype(jnp.float32)
                        + back_in[ready].astype(jnp.float32)
                    )

        return carry

    lax.fori_loop(0, max(least, units + gap * (levels + last)), step_at, 0)

    def drain(unit, carry):
        for level in range(levels):
            level_copy(unit, level).wait_send()
        if last > 0:

            @pl.when(s < last)
            def _():
                ahead_copy(unit).wait_send()

            @pl.when(s > 0)
            def _():
                back_copy(unit).wait_send()

        return carry

    lax.fori_loop(0, units, drain, 0)


def greet(plan):
    barrier = pltpu.get_barrier_semaphore()
    d = lax.axis_index("dp")
    s = lax.axis_index("seq")
    for level in range(plan.levels):
        step = 1 << level
        signal_to(barrier, {"dp": d + (1 - 2 * ((d // step) % 2)) * step})
    if plan.seq > 1:

        @pl.when(s > 0)
        def _():
            signal_to(barrier, {"seq": s - 1})

        @pl.when(s < plan.seq - 1)
        def _():
            signal_to(barrier, {"seq": s + 1})

    if plan.seq == 1:
        pl.semaphore_wait(barrier, plan.levels)
        return
    edge = jnp.logical_or(s == 0, s == plan.seq - 1)

    @pl.when(edge)
    def _():
        pl.semaphore_wait(barrier, plan.levels + 1)

    @pl.when(jnp.logical_not(edge))
    def _():
        pl.semaphore_wait(barrier, plan.levels + 2)


def gradient_kernel(plan, cot_ref, att_ref, out_ref, *refs):
    greet(plan)
    refs[0][...] = jnp.transpose(cot_ref[...])
    for c in range(plan.chunks):
        refs[1][c] = att_ref[:, c * plan.chunk : (c + 1) * plan.chunk]
    gradient_loop(plan, refs, out_ref)


def reduced_gradient(upstream, attended):
    plan = Plan(
        upstream.shape[0], upstream.shape[1], attended.shape[1],
        lax.axis_size("dp"), lax.axis_size("seq"),
    )
    whole = pl.BlockSpec(memory_space=pltpu.VMEM)
    return pl.pallas_call(
        functools.partial(gradient_kernel, plan),
        out_shape=jax.ShapeDtypeStruct((plan.block, plan.columns), jnp.float32),
        in_specs=[whole, whole],
        out_specs=whole,
        scratch_shapes=plan.scratch(),
        compiler_params=pltpu.CompilerParams(
            collective_id=0, has_side_effects=True, vmem_limit_bytes=56 * 2**20
        ),
        name="reduced_gradient",
    )(upstream, attended)


def meet(plan):
    barrier = pltpu.get_barrier_semaphore()
    d = lax.axis_index("dp")
    s = lax.axis_index("seq")
    for level in range(plan.levels):
        step = 1 << level
        signal_to(barrier, {"dp": d + (1 - 2 * ((d // step) % 2)) * step})
    for j in range(1, plan.seq):
        signal_to(barrier, {"seq": (s + j) % plan.seq})
    pl.semaphore_wait(barrier, plan.levels + plan.seq - 1)


EDGE = 16
TILE = 256


def section_kernel(plan, *refs):
    (x_hbm, conv_hbm, bias, gain, query_hbm, key_hbm, value_hbm, out_hbm, cot_hbm, turn_hbm) = refs[:10]
    mixed, grad_out = refs[10:12]
    (
        x_rows, conv_w, query_w, key_w, value_w, out_w, cot, turn, fetched,
        edges, edge_sems, spread, stacked, pooled, normed, queries, keys, values, kv_sems,
    ) = refs[12:31]
    gradient_refs = refs[31:]
    cot_t, att = gradient_refs[:2]
    tokens, rows = plan.tokens, 2 * plan.tokens
    s = lax.axis_index("seq")
    last = plan.seq - 1
    tiles = plan.width // TILE
    taps, channels = KERNEL_TAPS, x_rows.shape[1]

    def conv_fetch(n):
        return pltpu.make_async_copy(
            conv_hbm.at[:, pl.ds(pl.multiple_of(n * TILE, TILE), TILE)],
            conv_w.at[n],
            fetched.at[8 + n],
        )

    x_fetch = pltpu.make_async_copy(x_hbm, x_rows, fetched.at[0])
    key_fetch = pltpu.make_async_copy(key_hbm, key_w, fetched.at[1])
    value_fetch = pltpu.make_async_copy(value_hbm, value_w, fetched.at[2])
    turn_fetch = pltpu.make_async_copy(
        turn_hbm.at[pl.ds(pl.multiple_of(s * tokens, tokens), tokens)], turn, fetched.at[3]
    )
    query_fetch = pltpu.make_async_copy(query_hbm, query_w, fetched.at[4])
    cot_fetch = pltpu.make_async_copy(cot_hbm, cot, fetched.at[5])
    out_fetch = pltpu.make_async_copy(out_hbm, out_w, fetched.at[6])
    x_fetch.start()
    for n in range(tiles):
        conv_fetch(n).start()
    for fetch in (key_fetch, value_fetch, turn_fetch, query_fetch, cot_fetch, out_fetch):
        fetch.start()

    meet(plan)

    def edge_ahead():
        return remote(
            x_hbm.at[pl.ds(rows - EDGE, EDGE)], edges.at[0], edge_sems.at[0], edge_sems.at[1],
            {"seq": s + 1},
        )

    def edge_back():
        return remote(
            x_hbm.at[pl.ds(0, EDGE)], edges.at[1], edge_sems.at[2], edge_sems.at[3],
            {"seq": s - 1},
        )

    blocks = channels // 128
    if last > 0:

        @pl.when(s < last)
        def _():
            edge_ahead().start()

        @pl.when(s > 0)
        def _():
            edge_back().start()

    x_fetch.wait()
    for j in range(blocks):
        spread[j, EDGE : EDGE + rows, :] = x_rows[:, j * 128 : (j + 1) * 128].astype(jnp.float32)
    blank = jnp.zeros((EDGE, 128), jnp.float32)

    def put_edge(which, start, there):
        @pl.when(there)
        def _():
            if last > 0:
                (edge_ahead if which == 0 else edge_back)().wait_recv()
                for j in range(blocks):
                    spread[j, start : start + EDGE, :] = edges[
                        which, :, j * 128 : (j + 1) * 128
                    ].astype(jnp.float32)

        @pl.when(jnp.logical_not(there))
        def _():
            for j in range(blocks):
                spread[j, start : start + EDGE, :] = blank

    put_edge(0, 0, s > 0)
    put_edge(1, EDGE + rows, s < last)
    for parity in range(2):
        for tap in range(taps):
            for j in range(blocks):
                start = EDGE + parity + DILATION_STEP * (tap - 1)
                lane = tap * channels + j * 128
                stacked[parity * tokens : (parity + 1) * tokens, lane : lane + 128] = spread[
                    j, pl.ds(start, tokens, stride=2), :
                ].astype(jnp.bfloat16)

    def conv_tile(n, carry):
        conv_fetch(n).wait()
        columns = pl.ds(pl.multiple_of(n * TILE, TILE), TILE)
        pre = (
            jnp.dot(stacked[...], conv_w[n], preferred_element_type=jnp.float32)
            + bias[:, columns]
        )
        inner = math.sqrt(2.0 / math.pi) * (pre + 0.044715 * (pre * pre * pre))
        activated = pre * (0.5 * (1.0 + jnp.tanh(inner)))
        pooled[:, columns] = jnp.maximum(activated[:tokens], activated[tokens:]).astype(
            jnp.bfloat16
        )
        return carry

    lax.fori_loop(0, tiles, conv_tile, 0)

    part = 32

    def norm_part(i, carry):
        here = pl.ds(pl.multiple_of(i * part, part), part)
        wide = pooled[here, :].astype(jnp.float32)
        squares = jnp.mean(wide * wide, axis=-1, keepdims=True)
        normed[here, :] = (wide * lax.rsqrt(squares + norm_eps) * gain[...]).astype(jnp.bfloat16)
        return carry

    lax.fori_loop(0, tokens // part, norm_part, 0)

    key_fetch.wait()
    value_fetch.wait()
    turn_fetch.wait()

    def turned(vectors):
        return (
            vectors * turn[:, :KEY] + pltpu.roll(vectors, KEY // 2, 1) * turn[:, KEY:]
        ).astype(jnp.bfloat16)

    keys[s] = turned(jnp.dot(normed[...], key_w[...], preferred_element_type=jnp.float32))
    values[s] = jnp.dot(normed[...], value_w[...], preferred_element_type=jnp.float32).astype(
        jnp.bfloat16
    )

    def kv_copies(owner, j, peer):
        at = 4 * (j - 1)
        return (
            remote(keys.at[owner], keys.at[owner], kv_sems.at[at], kv_sems.at[at + 1], {"seq": peer}),
            remote(
                values.at[owner], values.at[owner], kv_sems.at[at + 2], kv_sems.at[at + 3],
                {"seq": peer},
            ),
        )

    for j in range(1, plan.seq):
        for copy in kv_copies(s, j, (s + j) % plan.seq):
            copy.start()

    query_fetch.wait()

    def query_pair(c, carry):
        pair = jnp.dot(
            normed[...],
            query_w[:, pl.ds(pl.multiple_of(c * 2 * KEY, 2 * KEY), 2 * KEY)],
            preferred_element_type=jnp.float32,
        )
        queries[2 * c] = turned(pair[:, :KEY])
        queries[2 * c + 1] = turned(pair[:, KEY:])
        return carry

    lax.fori_loop(0, plan.chunks, query_pair, 0)
    cot_fetch.wait()
    cot_t[...] = jnp.transpose(cot[...])
    out_fetch.wait()
    for j in range(1, plan.seq):
        owner = (s + plan.seq - j) % plan.seq
        for copy in kv_copies(owner, j, (s + j) % plan.seq):
            copy.wait_recv()

    def attend_head(h):
        scores = lax.dot_general(
            queries[h],
            keys[...].reshape(plan.seq * tokens, KEY),
            (((1,), (1,)), ((), ())),
            preferred_element_type=jnp.float32,
        )
        peak = jnp.max(scores, axis=-1, keepdims=True)
        weights = jnp.exp2((scores - peak) * (KEY ** (-0.5) * math.log2(math.e)))
        total = jnp.sum(weights, axis=-1, keepdims=True)
        weighted = jnp.dot(
            weights.astype(jnp.bfloat16),
            values[...].reshape(plan.seq * tokens, VAL),
            preferred_element_type=jnp.float32,
        )
        return weighted / total

    def produce(t):
        @pl.when(jnp.logical_and(t < plan.units, t % plan.pieces == 0))
        def _():
            c = t // plan.pieces
            att[c] = jnp.concatenate([attend_head(2 * c), attend_head(2 * c + 1)], axis=1).astype(
                jnp.bfloat16
            )

        @pl.when(jnp.logical_and(t >= plan.units, t < plan.units + tiles))
        def _():
            columns = pl.ds(pl.multiple_of((t - plan.units) * TILE, TILE), TILE)
            total = pooled[:, columns].astype(jnp.float32)
            for c in range(plan.chunks):
                total = total + jnp.dot(
                    att[c],
                    out_w[c * plan.chunk : (c + 1) * plan.chunk, columns],
                    preferred_element_type=jnp.float32,
                )
            mixed[:, columns] = total.astype(jnp.bfloat16)

    gradient_loop(plan, gradient_refs, grad_out, produce, plan.units + tiles)

    for j in range(1, plan.seq):
        for copy in kv_copies(s, j, (s + j) % plan.seq):
            copy.wait_send()
    if last > 0:

        @pl.when(s < last)
        def _():
            edge_ahead().wait_send()

        @pl.when(s > 0)
        def _():
            edge_back().wait_send()


def turn_table(count):
    frequency = np.exp(
        np.float32(-math.log(rope_base) * 2.0) * np.arange(KEY // 2, dtype=np.float32) / KEY
    ).astype(np.float32)
    angles = np.arange(count, dtype=np.float32)[:, None] * frequency[None, :]
    cosine, sines = np.cos(angles), np.sin(angles)
    return np.concatenate([cosine, cosine, -sines, sines], axis=1).astype(np.float32)


def section(x_in, kernel_weight, conv_bias, norm_gain, w_query, w_key, w_value, w_out, cotangent):
    inputs, upstream = x_in[0], cotangent[0]
    rows, channels = inputs.shape
    width = kernel_weight.shape[2]
    plan = Plan(
        rows // 2, width, w_out.shape[0], lax.axis_size("dp"), lax.axis_size("seq")
    )
    tokens, seq, tiles = plan.tokens, plan.seq, width // TILE
    depth = KERNEL_TAPS * channels
    bf = jnp.bfloat16
    held = pl.BlockSpec(memory_space=pltpu.VMEM)
    away = pl.BlockSpec(memory_space=pl.ANY)
    mixed, gradient = pl.pallas_call(
        functools.partial(section_kernel, plan),
        out_shape=(
            jax.ShapeDtypeStruct((tokens, width), bf),
            jax.ShapeDtypeStruct((plan.block, plan.columns), jnp.float32),
        ),
        in_specs=[away, away, held, held, away, away, away, away, away, away],
        out_specs=(held, held),
        scratch_shapes=[
            pltpu.VMEM((rows, channels), bf),
            pltpu.VMEM((tiles, depth, TILE), bf),
            pltpu.VMEM(w_query.shape, bf),
            pltpu.VMEM(w_key.shape, bf),
            pltpu.VMEM(w_value.shape, bf),
            pltpu.VMEM(w_out.shape, bf),
            pltpu.VMEM((tokens, width), bf),
            pltpu.VMEM((tokens, 2 * KEY), jnp.float32),
            pltpu.SemaphoreType.DMA((8 + tiles,)),
            pltpu.VMEM((2, EDGE, channels), bf),
            pltpu.SemaphoreType.DMA((4,)),
            pltpu.VMEM((channels // 128, rows + 2 * EDGE, 128), jnp.float32),
            pltpu.VMEM((rows, depth), bf),
            pltpu.VMEM((tokens, width), bf),
            pltpu.VMEM((tokens, width), bf),
            pltpu.VMEM((w_query.shape[1] // KEY, tokens, KEY), bf),
            pltpu.VMEM((seq, tokens, KEY), bf),
            pltpu.VMEM((seq, tokens, VAL), bf),
            pltpu.SemaphoreType.DMA((4 * max(seq - 1, 1),)),
        ]
        + plan.scratch(),
        compiler_params=pltpu.CompilerParams(
            collective_id=1, has_side_effects=True, vmem_limit_bytes=60 * 2**20
        ),
        name="section",
    )(
        inputs,
        kernel_weight.reshape(depth, width),
        conv_bias[None],
        norm_gain[None],
        w_query,
        w_key,
        w_value,
        w_out,
        upstream,
        turn_table(tokens * seq),
    )
    return mixed[None], gradient


def local(x_in, kernel_weight, conv_bias, norm_gain, w_query, w_key, w_value, w_out, cotangent):
    inputs = x_in[0]
    edge_padding = DILATION_STEP * (KERNEL_TAPS - 1) // 2
    padded_rows = padded(inputs, (("seq", 0),), edge_padding)
    padded_row_count = inputs.shape[0]
    before_activation = jnp.broadcast_to(
        conv_bias[None, :], (padded_row_count, kernel_weight.shape[2])
    )
    for kernel_tap_index in range(KERNEL_TAPS):
        before_activation = before_activation + jnp.dot(
            padded_rows[
                kernel_tap_index * DILATION_STEP : kernel_tap_index * DILATION_STEP
                + padded_row_count
            ],
            kernel_weight[kernel_tap_index],
            preferred_element_type=jnp.float32,
        )
    activated = jax.nn.gelu(before_activation)
    pooled = jnp.max(activated.reshape(padded_row_count // 2, 2, -1), axis=1).astype(jnp.bfloat16)
    token_count = pooled.shape[0]
    features = lax.all_gather(pooled, "head", axis=1, tiled=True)
    widened = features.astype(jnp.float32)
    squares = jnp.mean(widened * widened, axis=-1, keepdims=True)
    normed = (widened * lax.rsqrt(squares + norm_eps) * norm_gain).astype(jnp.bfloat16)
    seq_offset = lax.axis_index("seq") * token_count
    positions = seq_offset + jnp.arange(token_count, dtype=jnp.int32)
    local_heads = w_query.shape[1] // KEY
    queries = rotate(
        jnp.dot(normed, w_query, preferred_element_type=jnp.float32).reshape(
            token_count, local_heads, KEY
        ),
        positions,
    ).astype(jnp.bfloat16)
    own_rows = token_count // lax.axis_size("head")
    row_offset = lax.axis_index("head") * own_rows
    own_normed = lax.dynamic_slice_in_dim(normed, row_offset, own_rows, 0)
    own_positions = seq_offset + row_offset + jnp.arange(own_rows, dtype=jnp.int32)
    key_rows = rotate(
        jnp.dot(own_normed, w_key, preferred_element_type=jnp.float32), own_positions
    ).astype(jnp.bfloat16)
    value_rows = jnp.dot(own_normed, w_value, preferred_element_type=jnp.float32).astype(
        jnp.bfloat16
    )
    start_state = (
        jnp.full((local_heads, token_count), -1e30, jnp.float32),
        jnp.zeros((local_heads, token_count), jnp.float32),
        jnp.zeros((token_count, local_heads, VAL), jnp.float32),
    )
    both = lax.all_gather(
        jnp.concatenate([key_rows, value_rows], axis=1), ("seq", "head"), axis=0, tiled=True
    )
    final_state = attend_pieces(
        queries,
        both[:, :KEY],
        both[:, KEY:],
        start_state,
    )
    running_max, running_sum, weighted = final_state
    attended = (
        (weighted / jnp.transpose(running_sum)[:, :, None])
        .astype(jnp.bfloat16)
        .reshape(token_count, local_heads * VAL)
    )
    projected = lax.psum_scatter(
        lax.dot_general(
            w_out, attended, (((0,), (1,)), ((), ())), preferred_element_type=jnp.float32
        ).astype(jnp.bfloat16),
        "head",
        scatter_dimension=0,
        tiled=True,
    ).astype(jnp.float32)
    mixed = (pooled.astype(jnp.float32) + jnp.transpose(projected)).astype(jnp.bfloat16)[None]
    upstream = cotangent[0]
    gradient = reduced_gradient(upstream, attended)
    return (mixed, gradient)


def solution(mesh):
    return jax.shard_map(
        section if mesh.shape["head"] == 1 else local,
        mesh=mesh,
        in_specs=(
            P(("groups", "dp"), "seq", None),
            P(None, None, "head"),
            P("head"),
            P(),
            P(None, "head"),
            P(),
            P(),
            P("head", None),
            P(("groups", "dp"), "seq", None),
        ),
        out_specs=(P(("groups", "dp"), "seq", "head"), P(("groups", "dp"), "head")),
        check_vma=False,
    )
```

```python
import functools
import math

import jax
import jax.numpy as jnp
from jax import lax
from jax.experimental import pallas as pl
from jax.experimental.pallas import tpu as pltpu
import numpy as np
from jax.sharding import PartitionSpec as P

KEY = 128
VAL = 192
KERNEL_TAPS = 3
DILATION_STEP = 2


rope_base = 10000.0
norm_eps = 1e-06


def padded(cells, sides, width):
    for axis, dim in sides:
        count = lax.axis_size(axis)
        ends = count - 1
        head = lax.slice_in_dim(cells, 0, width, axis=dim)
        tail = lax.slice_in_dim(cells, cells.shape[dim] - width, cells.shape[dim], axis=dim)
        cells = jnp.concatenate(
            [
                lax.ppermute(tail, axis, [(i, (i + 1) % count) for i in range(ends)]),
                cells,
                lax.ppermute(head, axis, [((i + 1) % count, i) for i in range(ends)]),
            ],
            axis=dim,
        )
    return cells


def rotate(vectors, positions):
    halfway = vectors.shape[-1] // 2
    frequency = jnp.exp(
        -math.log(rope_base) * 2.0 * jnp.arange(halfway, dtype=jnp.float32) / vectors.shape[-1]
    )
    angles = positions.astype(jnp.float32)[:, None] * frequency[None, :]
    layout = (positions.shape[0],) + (1,) * (vectors.ndim - 2) + (halfway,)
    cosine = jnp.cos(angles).reshape(layout)
    sines = jnp.sin(angles).reshape(layout)
    leading = vectors[..., :halfway]
    trailing = vectors[..., halfway:]
    return jnp.concatenate(
        [leading * cosine - trailing * sines, leading * sines + trailing * cosine], axis=-1
    )


def attend_pieces(queries, key_rows, value_rows, state_in):
    total_keys = key_rows.shape[0]
    block_size = math.gcd(total_keys, 512)

    def one_block(block_index, state):
        running_max, running_sum, weighted = state
        key_block = lax.dynamic_slice_in_dim(key_rows, block_index * block_size, block_size, 0)
        value_block = lax.dynamic_slice_in_dim(value_rows, block_index * block_size, block_size, 0)
        scores = jnp.einsum(
            "thd,ud->htu", queries, key_block, preferred_element_type=jnp.float32
        ) * KEY ** (-0.5)
        new_max = jnp.maximum(running_max, jnp.max(scores, axis=-1))
        rescale = jnp.exp(running_max - new_max)
        weights = jnp.exp(scores - new_max[:, :, None])
        running_sum = running_sum * rescale + jnp.sum(weights, axis=-1)
        weighted = weighted * jnp.transpose(rescale)[:, :, None] + jnp.einsum(
            "htu,uv->thv",
            weights.astype(jnp.bfloat16),
            value_block,
            preferred_element_type=jnp.float32,
        )
        return (new_max, running_sum, weighted)

    return lax.fori_loop(0, total_keys // block_size, one_block, state_in)


def signal_to(sem, where):
    pl.semaphore_signal(sem, inc=1, device_id=where, device_id_type=pl.DeviceIdType.MESH)


def remote(src, dst, send_sem, recv_sem, where):
    return pltpu.make_async_remote_copy(
        src_ref=src,
        dst_ref=dst,
        send_sem=send_sem,
        recv_sem=recv_sem,
        device_id=where,
        device_id_type=pl.DeviceIdType.MESH,
    )


class Plan:
    def __init__(self, tokens, width, columns, dp, seq):
        self.tokens, self.width, self.columns = tokens, width, columns
        self.dp, self.seq = dp, seq
        self.levels = dp.bit_length() - 1
        self.block = width // dp
        self.rows = 64 if self.block % 64 == 0 else self.block
        self.pieces = self.block // self.rows
        self.chunk = 2 * VAL
        self.chunks = columns // self.chunk
        self.units = self.chunks * self.pieces
        self.gap = 4

    def scratch(self):
        tile = (self.rows, self.chunk)
        self.slots = self.gap * self.levels + 1
        shapes = [
            pltpu.VMEM((self.pieces, self.dp * self.rows, self.tokens), jnp.bfloat16),
            pltpu.VMEM((self.chunks, self.tokens, self.chunk), jnp.bfloat16),
            pltpu.VMEM((self.units,) + tile, jnp.float32),
            pltpu.VMEM((self.slots, self.dp * self.rows, self.chunk), jnp.float32),
        ]
        sends = self.levels + 2
        for level in range(self.levels):
            held = self.dp >> (level + 1)
            shapes += [pltpu.VMEM((self.units, held) + tile, jnp.bfloat16)] * 2
        shapes += [pltpu.VMEM((self.units,) + tile, jnp.bfloat16)] * 4
        shapes += [pltpu.SemaphoreType.DMA((self.units,))] * (2 * sends)
        return shapes


def turn_over(plan, cot_ref, cot_t):
    for piece in range(plan.pieces):
        for p in range(plan.dp):
            start = p * plan.block + piece * plan.rows
            cot_t[piece, p * plan.rows : (p + 1) * plan.rows, :] = jnp.transpose(
                cot_ref[:, start : start + plan.rows]
            )


def gradient_loop(plan, refs, out_ref, produce=None, least=0):
    cot_t, att, own, products = refs[:4]
    refs = refs[1:]
    levels, units = plan.levels, plan.units
    pairs = refs[3 : 3 + 2 * levels]
    ahead_out, ahead_in, back_out, back_in = refs[3 + 2 * levels : 7 + 2 * levels]
    sems = refs[7 + 2 * levels :]
    d = lax.axis_index("dp")
    s = lax.axis_index("seq")
    gap = plan.gap
    last = plan.seq - 1

    def summed(unit, p, level):
        start = pl.multiple_of(p * plan.rows, plan.rows)
        value = products[unit % plan.slots, pl.ds(start, plan.rows), :]
        for done in range(level):
            value = value + pairs[2 * done + 1][unit, p // (2 << done)].astype(jnp.float32)
        return value

    def level_copy(unit, level):
        step = 1 << level
        peer = d + (1 - 2 * ((d // step) % 2)) * step
        return remote(
            pairs[2 * level].at[unit],
            pairs[2 * level + 1].at[unit],
            sems[2 * level].at[unit],
            sems[2 * level + 1].at[unit],
            {"dp": peer},
        )

    def ahead_copy(unit):
        at = 2 * levels
        return remote(
            ahead_out.at[unit], ahead_in.at[unit], sems[at].at[unit], sems[at + 1].at[unit],
            {"seq": s + 1},
        )

    def back_copy(unit):
        at = 2 * levels + 2
        return remote(
            back_out.at[unit], back_in.at[unit], sems[at].at[unit], sems[at + 1].at[unit],
            {"seq": s - 1},
        )

    def within(unit):
        return jnp.logical_and(unit >= 0, unit < units)

    def step_at(t, carry):
        if produce is not None:
            produce(t)
        for level in range(levels):
            unit = t - gap * level

            @pl.when(within(unit))
            def _(unit=unit, level=level):
                if level == 0:
                    products[unit % plan.slots] = jnp.dot(
                        cot_t[unit % plan.pieces],
                        att[unit // plan.pieces],
                        preferred_element_type=jnp.float32,
                    )
                else:
                    level_copy(unit, level - 1).wait_recv()
                step = 1 << level
                base = d % step + (1 - (d // step) % 2) * step
                for i in range(plan.dp >> (level + 1)):
                    pairs[2 * level][unit, i] = summed(unit, base + i * 2 * step, level).astype(
                        jnp.bfloat16
                    )
                level_copy(unit, level).start()

        unit = t - gap * levels

        @pl.when(within(unit))
        def _():
            if levels > 0:
                level_copy(unit, levels - 1).wait_recv()
            else:
                products[unit % plan.slots] = jnp.dot(
                    cot_t[unit % plan.pieces],
                    att[unit // plan.pieces],
                    preferred_element_type=jnp.float32,
                )
            own[unit] = summed(unit, d, levels)

        if last > 0:
            fore = t - gap * (levels + s)

            @pl.when(jnp.logical_and(within(fore), s == 0))
            def _():
                ahead_out[fore] = own[fore].astype(jnp.bfloat16)
                ahead_copy(fore).start()

            @pl.when(jnp.logical_and(within(fore), s > 0))
            def _():
                ahead_copy(fore).wait_recv()

                @pl.when(s < last)
                def _():
                    ahead_out[fore] = (own[fore] + ahead_in[fore].astype(jnp.float32)).astype(
                        jnp.bfloat16
                    )
                    ahead_copy(fore).start()

            rear = t - gap * (levels + last - s)

            @pl.when(jnp.logical_and(within(rear), s == last))
            def _():
                back_out[rear] = own[rear].astype(jnp.bfloat16)
                back_copy(rear).start()

            @pl.when(jnp.logical_and(within(rear), s < last))
            def _():
                back_copy(rear).wait_recv()

                @pl.when(s > 0)
                def _():
                    back_out[rear] = (own[rear] + back_in[rear].astype(jnp.float32)).astype(
                        jnp.bfloat16
                    )
                    back_copy(rear).start()

        ready = t - gap * (levels + last)

        def store(value):
            row = pl.multiple_of((ready % plan.pieces) * plan.rows, plan.rows)
            column = pl.multiple_of((ready // plan.pieces) * plan.chunk, plan.chunk)
            out_ref[pl.ds(row, plan.rows), pl.ds(column, plan.chunk)] = value

        if last == 0:

            @pl.when(within(ready))
            def _():
                store(own[ready])

        else:

            @pl.when(jnp.logical_and(within(ready), s == 0))
            def _():
                store(own[ready] + back_in[ready].astype(jnp.float32))

            @pl.when(jnp.logical_and(within(ready), s == last))
            def _():
                store(own[ready] + ahead_in[ready].astype(jnp.float32))

            if last > 1:

                @pl.when(
                    jnp.logical_and(within(ready), jnp.logical_and(s > 0, s < last))
                )
                def _():
                    store(
                        own[ready]
                        + ahead_in[ready].astype(jnp.float32)
                        + back_in[ready].astype(jnp.float32)
                    )

        return carry

    lax.fori_loop(0, max(least, units + gap * (levels + last)), step_at, 0)

    def drain(unit, carry):
        for level in range(levels):
            level_copy(unit, level).wait_send()
        if last > 0:

            @pl.when(s < last)
            def _():
                ahead_copy(unit).wait_send()

            @pl.when(s > 0)
            def _():
                back_copy(unit).wait_send()

        return carry

    lax.fori_loop(0, units, drain, 0)


def greet(plan):
    barrier = pltpu.get_barrier_semaphore()
    d = lax.axis_index("dp")
    s = lax.axis_index("seq")
    for level in range(plan.levels):
        step = 1 << level
        signal_to(barrier, {"dp": d + (1 - 2 * ((d // step) % 2)) * step})
    if plan.seq > 1:

        @pl.when(s > 0)
        def _():
            signal_to(barrier, {"seq": s - 1})

        @pl.when(s < plan.seq - 1)
        def _():
            signal_to(barrier, {"seq": s + 1})

    if plan.seq == 1:
        pl.semaphore_wait(barrier, plan.levels)
        return
    edge = jnp.logical_or(s == 0, s == plan.seq - 1)

    @pl.when(edge)
    def _():
        pl.semaphore_wait(barrier, plan.levels + 1)

    @pl.when(jnp.logical_not(edge))
    def _():
        pl.semaphore_wait(barrier, plan.levels + 2)


def gradient_kernel(plan, cot_ref, att_ref, out_ref, *refs):
    greet(plan)
    turn_over(plan, cot_ref, refs[0])
    for c in range(plan.chunks):
        refs[1][c] = att_ref[:, c * plan.chunk : (c + 1) * plan.chunk]
    gradient_loop(plan, refs, out_ref)


def reduced_gradient(upstream, attended):
    plan = Plan(
        upstream.shape[0], upstream.shape[1], attended.shape[1],
        lax.axis_size("dp"), lax.axis_size("seq"),
    )
    whole = pl.BlockSpec(memory_space=pltpu.VMEM)
    return pl.pallas_call(
        functools.partial(gradient_kernel, plan),
        out_shape=jax.ShapeDtypeStruct((plan.block, plan.columns), jnp.float32),
        in_specs=[whole, whole],
        out_specs=whole,
        scratch_shapes=plan.scratch(),
        compiler_params=pltpu.CompilerParams(
            collective_id=0, has_side_effects=True, vmem_limit_bytes=56 * 2**20
        ),
        name="reduced_gradient",
    )(upstream, attended)


EDGE = 16
TILE = 256


def section_kernel(plan, *refs):
    (x_hbm, conv_hbm, bias_in, gain_in, query_hbm, key_hbm, value_hbm, out_hbm, cot_hbm, turn_hbm) = refs[:10]
    mixed, grad_out = refs[10:12]
    (
        x_rows, conv_w, query_w, key_w, value_w, out_w, cot, turn, fetched,
        edges, edge_sems, spread, stacked, pooled, normed, queries, kv, values, kv_sems, bias, gain,
    ) = refs[12:33]
    gradient_refs = refs[33:]
    cot_t, att = gradient_refs[:2]
    tokens, rows = plan.tokens, 2 * plan.tokens
    s = lax.axis_index("seq")
    last = plan.seq - 1
    tiles = plan.width // TILE
    taps, channels = KERNEL_TAPS, x_rows.shape[1]

    def conv_fetch(n):
        return pltpu.make_async_copy(
            conv_hbm.at[:, pl.ds(pl.multiple_of(n * TILE, TILE), TILE)],
            conv_w.at[n],
            fetched.at[8 + n],
        )

    x_fetch = pltpu.make_async_copy(x_hbm, x_rows, fetched.at[0])
    key_fetch = pltpu.make_async_copy(key_hbm, key_w, fetched.at[1])
    value_fetch = pltpu.make_async_copy(value_hbm, value_w, fetched.at[2])
    turn_fetch = pltpu.make_async_copy(
        turn_hbm.at[pl.ds(pl.multiple_of(s * tokens, tokens), tokens)], turn, fetched.at[3]
    )
    query_fetch = pltpu.make_async_copy(query_hbm, query_w, fetched.at[4])
    cot_fetch = pltpu.make_async_copy(cot_hbm, cot, fetched.at[5])
    out_fetch = pltpu.make_async_copy(out_hbm, out_w, fetched.at[6])
    x_fetch.start()
    for n in range(tiles):
        conv_fetch(n).start()
    for fetch in (key_fetch, value_fetch, turn_fetch, query_fetch, cot_fetch, out_fetch):
        fetch.start()

    bias[...] = bias_in[...].reshape(bias.shape)
    gain[...] = gain_in[...].reshape(gain.shape)
    greet(plan)

    def edge_ahead():
        return remote(
            x_hbm.at[pl.ds(rows - EDGE, EDGE)], edges.at[0], edge_sems.at[0], edge_sems.at[1],
            {"seq": s + 1},
        )

    def edge_back():
        return remote(
            x_hbm.at[pl.ds(0, EDGE)], edges.at[1], edge_sems.at[2], edge_sems.at[3],
            {"seq": s - 1},
        )

    blocks = channels // 128
    if last > 0:

        @pl.when(s < last)
        def _():
            edge_ahead().start()

        @pl.when(s > 0)
        def _():
            edge_back().start()

    x_fetch.wait()
    for j in range(blocks):
        spread[j, EDGE : EDGE + rows, :] = x_rows[:, j * 128 : (j + 1) * 128].astype(jnp.float32)
    blank = jnp.zeros((EDGE, 128), jnp.float32)
    for j in range(blocks):
        spread[j, :EDGE, :] = blank
        spread[j, EDGE + rows :, :] = blank

    def stack(tap, first, count):
        for parity in range(2):
            for j in range(blocks):
                start = EDGE + parity + DILATION_STEP * (tap - 1) + 2 * first
                lane = tap * channels + j * 128
                row = parity * tokens + first
                stacked[row : row + count, lane : lane + 128] = spread[
                    j, pl.ds(start, count, stride=2), :
                ].astype(jnp.bfloat16)

    for tap in range(taps):
        stack(tap, 0, tokens)

    def put_edge(which, start, tap, first):
        (edge_ahead if which == 0 else edge_back)().wait_recv()
        for j in range(blocks):
            spread[j, start : start + EDGE, :] = edges[which, :, j * 128 : (j + 1) * 128].astype(
                jnp.float32
            )
        stack(tap, first, EDGE)

    if last > 0:

        @pl.when(s > 0)
        def _():
            put_edge(0, 0, 0, 0)

        @pl.when(s < last)
        def _():
            put_edge(1, EDGE + rows, taps - 1, tokens - EDGE)

    def conv_tile(n, carry):
        conv_fetch(n).wait()
        columns = pl.ds(pl.multiple_of(n * TILE, TILE), TILE)
        pre = (
            jnp.dot(stacked[...], conv_w[n], preferred_element_type=jnp.float32)
            + bias[:, columns]
        )
        inner = math.sqrt(2.0 / math.pi) * (pre + 0.044715 * (pre * pre * pre))
        activated = pre * (0.5 * (1.0 + jnp.tanh(inner)))
        pooled[:, columns] = jnp.maximum(activated[:tokens], activated[tokens:]).astype(
            jnp.bfloat16
        )
        return carry

    lax.fori_loop(0, tiles, conv_tile, 0)

    part = 32

    def norm_part(i, carry):
        here = pl.ds(pl.multiple_of(i * part, part), part)
        wide = pooled[here, :].astype(jnp.float32)
        squares = jnp.mean(wide * wide, axis=-1, keepdims=True)
        normed[here, :] = (wide * lax.rsqrt(squares + norm_eps) * gain[...]).astype(jnp.bfloat16)
        return carry

    lax.fori_loop(0, tokens // part, norm_part, 0)

    key_fetch.wait()
    value_fetch.wait()
    turn_fetch.wait()

    def turned(vectors):
        return (
            vectors * turn[:, :KEY] + pltpu.roll(vectors, KEY // 2, 1) * turn[:, KEY:]
        ).astype(jnp.bfloat16)

    half = tokens // 2
    kv[s, :tokens, :] = turned(
        jnp.dot(normed[...], key_w[...], preferred_element_type=jnp.float32)
    )
    own_values = lax.dot_general(
        normed[...], value_w[...], (((1,), (1,)), ((), ())), preferred_element_type=jnp.float32
    )
    kv[s, tokens : 2 * tokens, :] = own_values[:, :128].astype(jnp.bfloat16)
    kv[s, 2 * tokens :, :] = jnp.concatenate(
        [own_values[:half, 128:], own_values[half:, 128:]], axis=1
    ).astype(jnp.bfloat16)
    split = 5 * tokens // 4

    def kv_copy(way, hop, h):
        owner = s - hop if way == 0 else s + hop
        owner = jnp.clip(owner, 0, last)
        at = ((way * last + hop) * 2 + h) * 2
        block = kv.at[owner, pl.ds(h * split, split)]
        return remote(
            block, block, kv_sems.at[at], kv_sems.at[at + 1],
            {"seq": s + 1 if way == 0 else s - 1},
        )

    def kv_sent(way, hop):
        if way == 0:
            return jnp.logical_and(s >= hop, s < last)
        return jnp.logical_and(s + hop <= last, s > 0)

    for way in range(2) if last > 0 else ():

        @pl.when(kv_sent(way, 0))
        def _(way=way):
            kv_copy(way, 0, 0).start()
            kv_copy(way, 0, 1).start()

    query_fetch.wait()

    def query_pair(c, carry):
        pair = jnp.dot(
            normed[...],
            query_w[:, pl.ds(pl.multiple_of(c * 2 * KEY, 2 * KEY), 2 * KEY)],
            preferred_element_type=jnp.float32,
        )
        queries[2 * c] = turned(pair[:, :KEY])
        queries[2 * c + 1] = turned(pair[:, KEY:])
        return carry

    lax.fori_loop(0, plan.chunks, query_pair, 0)
    cot_fetch.wait()
    turn_over(plan, cot, cot_t)
    out_fetch.wait()
    for hop in range(last):
        for h in range(2):
            for way in range(2):
                got = s > hop if way == 0 else s + hop < last

                @pl.when(got)
                def _(hop=hop, h=h, way=way):
                    kv_copy(way, hop, h).wait_recv()

                    @pl.when(s < last if way == 0 else s > 0)
                    def _():
                        if hop + 1 < last:
                            kv_copy(way, hop + 1, h).start()

    for j in range(plan.seq):
        values[j, :, :128] = kv[j, tokens : 2 * tokens, :]
        values[j, :half, 128:] = kv[j, 2 * tokens :, : VAL - 128]
        values[j, half:, 128:] = kv[j, 2 * tokens :, VAL - 128 :]

    def attend_head(h):
        scores = lax.dot_general(
            queries[h],
            kv[:, :tokens, :].reshape(plan.seq * tokens, KEY),
            (((1,), (1,)), ((), ())),
            preferred_element_type=jnp.float32,
        )
        peak = jnp.max(scores, axis=-1, keepdims=True)
        weights = jnp.exp2((scores - peak) * (KEY ** (-0.5) * math.log2(math.e)))
        total = jnp.sum(weights, axis=-1, keepdims=True)
        weighted = jnp.dot(
            weights.astype(jnp.bfloat16),
            values[...].reshape(plan.seq * tokens, VAL),
            preferred_element_type=jnp.float32,
        )
        return weighted / total

    def produce(t):
        @pl.when(jnp.logical_and(t < plan.units, t % plan.pieces == 0))
        def _():
            c = t // plan.pieces
            att[c] = jnp.concatenate([attend_head(2 * c), attend_head(2 * c + 1)], axis=1).astype(
                jnp.bfloat16
            )

        @pl.when(jnp.logical_and(t >= plan.units, t < plan.units + tiles))
        def _():
            columns = pl.ds(pl.multiple_of((t - plan.units) * TILE, TILE), TILE)
            total = pooled[:, columns].astype(jnp.float32)
            for c in range(plan.chunks):
                total = total + jnp.dot(
                    att[c],
                    out_w[c * plan.chunk : (c + 1) * plan.chunk, columns],
                    preferred_element_type=jnp.float32,
                )
            mixed[:, columns] = total.astype(jnp.bfloat16)

    gradient_loop(plan, gradient_refs, grad_out, produce, plan.units + tiles)

    for hop in range(last):
        for way in range(2):

            @pl.when(kv_sent(way, hop))
            def _(hop=hop, way=way):
                kv_copy(way, hop, 0).wait_send()
                kv_copy(way, hop, 1).wait_send()

    if last > 0:

        @pl.when(s < last)
        def _():
            edge_ahead().wait_send()

        @pl.when(s > 0)
        def _():
            edge_back().wait_send()


def turn_table(count):
    frequency = np.exp(
        np.float32(-math.log(rope_base) * 2.0) * np.arange(KEY // 2, dtype=np.float32) / KEY
    ).astype(np.float32)
    angles = np.arange(count, dtype=np.float32)[:, None] * frequency[None, :]
    cosine, sines = np.cos(angles), np.sin(angles)
    return np.concatenate([cosine, cosine, -sines, sines], axis=1).astype(np.float32)


def section(x_in, kernel_weight, conv_bias, norm_gain, w_query, w_key, w_value, w_out, cotangent):
    inputs, upstream = x_in[0], cotangent[0]
    rows, channels = inputs.shape
    width = kernel_weight.shape[2]
    plan = Plan(
        rows // 2, width, w_out.shape[0], lax.axis_size("dp"), lax.axis_size("seq")
    )
    tokens, seq, tiles = plan.tokens, plan.seq, width // TILE
    depth = KERNEL_TAPS * channels
    bf = jnp.bfloat16
    held = pl.BlockSpec(memory_space=pltpu.VMEM)
    away = pl.BlockSpec(memory_space=pl.ANY)
    mixed, gradient = pl.pallas_call(
        functools.partial(section_kernel, plan),
        out_shape=(
            jax.ShapeDtypeStruct((tokens, width), bf),
            jax.ShapeDtypeStruct((plan.block, plan.columns), jnp.float32),
        ),
        in_specs=[away, away, held, held, away, away, away, away, away, away],
        out_specs=(held, held),
        scratch_shapes=[
            pltpu.VMEM((rows, channels), bf),
            pltpu.VMEM((tiles, depth, TILE), bf),
            pltpu.VMEM(w_query.shape, bf),
            pltpu.VMEM(w_key.shape, bf),
            pltpu.VMEM(w_value.shape[::-1], bf),
            pltpu.VMEM(w_out.shape, bf),
            pltpu.VMEM((tokens, width), bf),
            pltpu.VMEM((tokens, 2 * KEY), jnp.float32),
            pltpu.SemaphoreType.DMA((8 + tiles,)),
            pltpu.VMEM((2, EDGE, channels), bf),
            pltpu.SemaphoreType.DMA((4,)),
            pltpu.VMEM((channels // 128, rows + 2 * EDGE, 128), jnp.float32),
            pltpu.VMEM((rows, depth), bf),
            pltpu.VMEM((tokens, width), bf),
            pltpu.VMEM((tokens, width), bf),
            pltpu.VMEM((w_query.shape[1] // KEY, tokens, KEY), bf),
            pltpu.VMEM((seq, 5 * tokens // 2, KEY), bf),
            pltpu.VMEM((seq, tokens, VAL), bf),
            pltpu.SemaphoreType.DMA((8 * max(seq - 1, 1),)),
            pltpu.VMEM((1, width), jnp.float32),
            pltpu.VMEM((1, width), jnp.float32),
        ]
        + plan.scratch(),
        compiler_params=pltpu.CompilerParams(
            collective_id=1, has_side_effects=True, vmem_limit_bytes=60 * 2**20
        ),
        name="section",
    )(
        inputs,
        kernel_weight.reshape(depth, width),
        conv_bias,
        norm_gain,
        w_query,
        w_key,
        jnp.transpose(w_value),
        w_out,
        upstream,
        turn_table(tokens * seq),
    )
    return mixed[None], gradient


def local(x_in, kernel_weight, conv_bias, norm_gain, w_query, w_key, w_value, w_out, cotangent):
    inputs = x_in[0]
    edge_padding = DILATION_STEP * (KERNEL_TAPS - 1) // 2
    padded_rows = padded(inputs, (("seq", 0),), edge_padding)
    padded_row_count = inputs.shape[0]
    before_activation = jnp.broadcast_to(
        conv_bias[None, :], (padded_row_count, kernel_weight.shape[2])
    )
    for kernel_tap_index in range(KERNEL_TAPS):
        before_activation = before_activation + jnp.dot(
            padded_rows[
                kernel_tap_index * DILATION_STEP : kernel_tap_index * DILATION_STEP
                + padded_row_count
            ],
            kernel_weight[kernel_tap_index],
            preferred_element_type=jnp.float32,
        )
    activated = jax.nn.gelu(before_activation)
    pooled = jnp.max(activated.reshape(padded_row_count // 2, 2, -1), axis=1).astype(jnp.bfloat16)
    token_count = pooled.shape[0]
    features = lax.all_gather(pooled, "head", axis=1, tiled=True)
    widened = features.astype(jnp.float32)
    squares = jnp.mean(widened * widened, axis=-1, keepdims=True)
    normed = (widened * lax.rsqrt(squares + norm_eps) * norm_gain).astype(jnp.bfloat16)
    seq_offset = lax.axis_index("seq") * token_count
    positions = seq_offset + jnp.arange(token_count, dtype=jnp.int32)
    local_heads = w_query.shape[1] // KEY
    queries = rotate(
        jnp.dot(normed, w_query, preferred_element_type=jnp.float32).reshape(
            token_count, local_heads, KEY
        ),
        positions,
    ).astype(jnp.bfloat16)
    own_rows = token_count // lax.axis_size("head")
    row_offset = lax.axis_index("head") * own_rows
    own_normed = lax.dynamic_slice_in_dim(normed, row_offset, own_rows, 0)
    own_positions = seq_offset + row_offset + jnp.arange(own_rows, dtype=jnp.int32)
    key_rows = rotate(
        jnp.dot(own_normed, w_key, preferred_element_type=jnp.float32), own_positions
    ).astype(jnp.bfloat16)
    value_rows = jnp.dot(own_normed, w_value, preferred_element_type=jnp.float32).astype(
        jnp.bfloat16
    )
    start_state = (
        jnp.full((local_heads, token_count), -1e30, jnp.float32),
        jnp.zeros((local_heads, token_count), jnp.float32),
        jnp.zeros((token_count, local_heads, VAL), jnp.float32),
    )
    both = lax.all_gather(
        jnp.concatenate([key_rows, value_rows], axis=1), ("seq", "head"), axis=0, tiled=True
    )
    final_state = attend_pieces(
        queries,
        both[:, :KEY],
        both[:, KEY:],
        start_state,
    )
    running_max, running_sum, weighted = final_state
    attended = (
        (weighted / jnp.transpose(running_sum)[:, :, None])
        .astype(jnp.bfloat16)
        .reshape(token_count, local_heads * VAL)
    )
    projected = lax.psum_scatter(
        lax.dot_general(
            w_out, attended, (((0,), (1,)), ((), ())), preferred_element_type=jnp.float32
        ).astype(jnp.bfloat16),
        "head",
        scatter_dimension=0,
        tiled=True,
    ).astype(jnp.float32)
    mixed = (pooled.astype(jnp.float32) + jnp.transpose(projected)).astype(jnp.bfloat16)[None]
    upstream = cotangent[0]
    gradient = reduced_gradient(upstream, attended)
    return (mixed, gradient)


def solution(mesh):
    return jax.shard_map(
        section if mesh.shape["head"] == 1 else local,
        mesh=mesh,
        in_specs=(
            P(("groups", "dp"), "seq", None),
            P(None, None, "head"),
            P("head"),
            P(),
            P(None, "head"),
            P(),
            P(),
            P("head", None),
            P(("groups", "dp"), "seq", None),
        ),
        out_specs=(P(("groups", "dp"), "seq", "head"), P(("groups", "dp"), "head")),
        check_vma=False,
    )
```

```python
import functools
import math

import jax
import jax.numpy as jnp
from jax import lax
from jax.experimental import pallas as pl
from jax.experimental.pallas import tpu as pltpu
import numpy as np
from jax.sharding import PartitionSpec as P

KEY = 128
VAL = 192
KERNEL_TAPS = 3
DILATION_STEP = 2


rope_base = 10000.0
norm_eps = 1e-06


def padded(cells, sides, width):
    for axis, dim in sides:
        count = lax.axis_size(axis)
        ends = count - 1
        head = lax.slice_in_dim(cells, 0, width, axis=dim)
        tail = lax.slice_in_dim(cells, cells.shape[dim] - width, cells.shape[dim], axis=dim)
        cells = jnp.concatenate(
            [
                lax.ppermute(tail, axis, [(i, (i + 1) % count) for i in range(ends)]),
                cells,
                lax.ppermute(head, axis, [((i + 1) % count, i) for i in range(ends)]),
            ],
            axis=dim,
        )
    return cells


def rotate(vectors, positions):
    halfway = vectors.shape[-1] // 2
    frequency = jnp.exp(
        -math.log(rope_base) * 2.0 * jnp.arange(halfway, dtype=jnp.float32) / vectors.shape[-1]
    )
    angles = positions.astype(jnp.float32)[:, None] * frequency[None, :]
    layout = (positions.shape[0],) + (1,) * (vectors.ndim - 2) + (halfway,)
    cosine = jnp.cos(angles).reshape(layout)
    sines = jnp.sin(angles).reshape(layout)
    leading = vectors[..., :halfway]
    trailing = vectors[..., halfway:]
    return jnp.concatenate(
        [leading * cosine - trailing * sines, leading * sines + trailing * cosine], axis=-1
    )


def attend_pieces(queries, key_rows, value_rows, state_in):
    total_keys = key_rows.shape[0]
    block_size = math.gcd(total_keys, 512)

    def one_block(block_index, state):
        running_max, running_sum, weighted = state
        key_block = lax.dynamic_slice_in_dim(key_rows, block_index * block_size, block_size, 0)
        value_block = lax.dynamic_slice_in_dim(value_rows, block_index * block_size, block_size, 0)
        scores = jnp.einsum(
            "thd,ud->htu", queries, key_block, preferred_element_type=jnp.float32
        ) * KEY ** (-0.5)
        new_max = jnp.maximum(running_max, jnp.max(scores, axis=-1))
        rescale = jnp.exp(running_max - new_max)
        weights = jnp.exp(scores - new_max[:, :, None])
        running_sum = running_sum * rescale + jnp.sum(weights, axis=-1)
        weighted = weighted * jnp.transpose(rescale)[:, :, None] + jnp.einsum(
            "htu,uv->thv",
            weights.astype(jnp.bfloat16),
            value_block,
            preferred_element_type=jnp.float32,
        )
        return (new_max, running_sum, weighted)

    return lax.fori_loop(0, total_keys // block_size, one_block, state_in)


def signal_to(sem, where):
    pl.semaphore_signal(sem, inc=1, device_id=where, device_id_type=pl.DeviceIdType.MESH)


def remote(src, dst, send_sem, recv_sem, where):
    return pltpu.make_async_remote_copy(
        src_ref=src,
        dst_ref=dst,
        send_sem=send_sem,
        recv_sem=recv_sem,
        device_id=where,
        device_id_type=pl.DeviceIdType.MESH,
    )


class Plan:
    def __init__(self, tokens, width, columns, dp, seq):
        self.tokens, self.width, self.columns = tokens, width, columns
        self.dp, self.seq = dp, seq
        self.levels = dp.bit_length() - 1
        self.block = width // dp
        self.rows = 64 if self.block % 64 == 0 else self.block
        self.pieces = self.block // self.rows
        self.chunk = 2 * VAL
        self.chunks = columns // self.chunk
        self.units = self.chunks * self.pieces
        self.gap = 4

    def scratch(self):
        tile = (self.rows, self.chunk)
        self.slots = self.gap * self.levels + 1
        shapes = [
            pltpu.VMEM((self.pieces, self.dp * self.rows, self.tokens), jnp.bfloat16),
            pltpu.VMEM((self.chunks, self.tokens, self.chunk), jnp.bfloat16),
            pltpu.VMEM((self.units,) + tile, jnp.float32),
            pltpu.VMEM((self.slots, self.dp * self.rows, self.chunk), jnp.float32),
        ]
        sends = self.levels + 2
        for level in range(self.levels):
            held = self.dp >> (level + 1)
            shapes += [pltpu.VMEM((self.units, held) + tile, jnp.bfloat16)] * 2
        shapes += [pltpu.VMEM((self.units,) + tile, jnp.bfloat16)] * 4
        shapes += [pltpu.SemaphoreType.DMA((self.units,))] * (2 * sends)
        return shapes


def turn_over(plan, cot_ref, cot_t):
    for piece in range(plan.pieces):
        for p in range(plan.dp):
            start = p * plan.block + piece * plan.rows
            cot_t[piece, p * plan.rows : (p + 1) * plan.rows, :] = jnp.transpose(
                cot_ref[:, start : start + plan.rows]
            )


def gradient_loop(plan, refs, out_ref, produce=None, least=0):
    cot_t, att, own, products = refs[:4]
    refs = refs[1:]
    levels, units = plan.levels, plan.units
    pairs = refs[3 : 3 + 2 * levels]
    ahead_out, ahead_in, back_out, back_in = refs[3 + 2 * levels : 7 + 2 * levels]
    sems = refs[7 + 2 * levels :]
    d = lax.axis_index("dp")
    s = lax.axis_index("seq")
    gap = plan.gap
    last = plan.seq - 1

    def summed(unit, p, level):
        start = pl.multiple_of(p * plan.rows, plan.rows)
        value = products[unit % plan.slots, pl.ds(start, plan.rows), :]
        for done in range(level):
            value = value + pairs[2 * done + 1][unit, p // (2 << done)].astype(jnp.float32)
        return value

    def level_copy(unit, level):
        step = 1 << level
        peer = d + (1 - 2 * ((d // step) % 2)) * step
        return remote(
            pairs[2 * level].at[unit],
            pairs[2 * level + 1].at[unit],
            sems[2 * level].at[unit],
            sems[2 * level + 1].at[unit],
            {"dp": peer},
        )

    def ahead_copy(unit):
        at = 2 * levels
        return remote(
            ahead_out.at[unit], ahead_in.at[unit], sems[at].at[unit], sems[at + 1].at[unit],
            {"seq": s + 1},
        )

    def back_copy(unit):
        at = 2 * levels + 2
        return remote(
            back_out.at[unit], back_in.at[unit], sems[at].at[unit], sems[at + 1].at[unit],
            {"seq": s - 1},
        )

    def within(unit):
        return jnp.logical_and(unit >= 0, unit < units)

    def step_at(t, carry):
        if produce is not None:
            produce(t)
        for level in range(levels):
            unit = t - gap * level

            @pl.when(within(unit))
            def _(unit=unit, level=level):
                if level == 0:
                    products[unit % plan.slots] = jnp.dot(
                        cot_t[unit % plan.pieces],
                        att[unit // plan.pieces],
                        preferred_element_type=jnp.float32,
                    )
                else:
                    level_copy(unit, level - 1).wait_recv()
                step = 1 << level
                base = d % step + (1 - (d // step) % 2) * step
                for i in range(plan.dp >> (level + 1)):
                    pairs[2 * level][unit, i] = summed(unit, base + i * 2 * step, level).astype(
                        jnp.bfloat16
                    )
                level_copy(unit, level).start()

        unit = t - gap * levels

        @pl.when(within(unit))
        def _():
            if levels > 0:
                level_copy(unit, levels - 1).wait_recv()
            else:
                products[unit % plan.slots] = jnp.dot(
                    cot_t[unit % plan.pieces],
                    att[unit // plan.pieces],
                    preferred_element_type=jnp.float32,
                )
            own[unit] = summed(unit, d, levels)

        if last > 0:
            fore = t - gap * (levels + s)

            @pl.when(jnp.logical_and(within(fore), s == 0))
            def _():
                ahead_out[fore] = own[fore].astype(jnp.bfloat16)
                ahead_copy(fore).start()

            @pl.when(jnp.logical_and(within(fore), s > 0))
            def _():
                ahead_copy(fore).wait_recv()

                @pl.when(s < last)
                def _():
                    ahead_out[fore] = (own[fore] + ahead_in[fore].astype(jnp.float32)).astype(
                        jnp.bfloat16
                    )
                    ahead_copy(fore).start()

            rear = t - gap * (levels + last - s)

            @pl.when(jnp.logical_and(within(rear), s == last))
            def _():
                back_out[rear] = own[rear].astype(jnp.bfloat16)
                back_copy(rear).start()

            @pl.when(jnp.logical_and(within(rear), s < last))
            def _():
                back_copy(rear).wait_recv()

                @pl.when(s > 0)
                def _():
                    back_out[rear] = (own[rear] + back_in[rear].astype(jnp.float32)).astype(
                        jnp.bfloat16
                    )
                    back_copy(rear).start()

        ready = t - gap * (levels + last)

        def store(value):
            row = pl.multiple_of((ready % plan.pieces) * plan.rows, plan.rows)
            column = pl.multiple_of((ready // plan.pieces) * plan.chunk, plan.chunk)
            out_ref[pl.ds(row, plan.rows), pl.ds(column, plan.chunk)] = value.astype(out_ref.dtype)

        if last == 0:

            @pl.when(within(ready))
            def _():
                store(own[ready])

        else:

            @pl.when(jnp.logical_and(within(ready), s == 0))
            def _():
                store(own[ready] + back_in[ready].astype(jnp.float32))

            @pl.when(jnp.logical_and(within(ready), s == last))
            def _():
                store(own[ready] + ahead_in[ready].astype(jnp.float32))

            if last > 1:

                @pl.when(
                    jnp.logical_and(within(ready), jnp.logical_and(s > 0, s < last))
                )
                def _():
                    store(
                        own[ready]
                        + ahead_in[ready].astype(jnp.float32)
                        + back_in[ready].astype(jnp.float32)
                    )

        return carry

    lax.fori_loop(0, max(least, units + gap * (levels + last)), step_at, 0)

    def drain(unit, carry):
        for level in range(levels):
            level_copy(unit, level).wait_send()
        if last > 0:

            @pl.when(s < last)
            def _():
                ahead_copy(unit).wait_send()

            @pl.when(s > 0)
            def _():
                back_copy(unit).wait_send()

        return carry

    lax.fori_loop(0, units, drain, 0)


def greet(plan):
    barrier = pltpu.get_barrier_semaphore()
    d = lax.axis_index("dp")
    s = lax.axis_index("seq")
    for level in range(plan.levels):
        step = 1 << level
        signal_to(barrier, {"dp": d + (1 - 2 * ((d // step) % 2)) * step})
    if plan.seq > 1:

        @pl.when(s > 0)
        def _():
            signal_to(barrier, {"seq": s - 1})

        @pl.when(s < plan.seq - 1)
        def _():
            signal_to(barrier, {"seq": s + 1})

    if plan.seq == 1:
        pl.semaphore_wait(barrier, plan.levels)
        return
    edge = jnp.logical_or(s == 0, s == plan.seq - 1)

    @pl.when(edge)
    def _():
        pl.semaphore_wait(barrier, plan.levels + 1)

    @pl.when(jnp.logical_not(edge))
    def _():
        pl.semaphore_wait(barrier, plan.levels + 2)


def gradient_kernel(plan, cot_ref, att_ref, out_ref, *refs):
    greet(plan)
    turn_over(plan, cot_ref, refs[0])
    for c in range(plan.chunks):
        refs[1][c] = att_ref[:, c * plan.chunk : (c + 1) * plan.chunk]
    gradient_loop(plan, refs, out_ref)


def reduced_gradient(upstream, attended):
    plan = Plan(
        upstream.shape[0], upstream.shape[1], attended.shape[1],
        lax.axis_size("dp"), lax.axis_size("seq"),
    )
    whole = pl.BlockSpec(memory_space=pltpu.VMEM)
    return pl.pallas_call(
        functools.partial(gradient_kernel, plan),
        out_shape=jax.ShapeDtypeStruct((plan.block, plan.columns), jnp.float32),
        in_specs=[whole, whole],
        out_specs=whole,
        scratch_shapes=plan.scratch(),
        compiler_params=pltpu.CompilerParams(
            collective_id=0, has_side_effects=True, vmem_limit_bytes=56 * 2**20
        ),
        name="reduced_gradient",
    )(upstream, attended)


EDGE = 16
TILE = 256


def section_kernel(plan, *refs):
    (x_hbm, conv_hbm, bias_in, gain_in, query_hbm, key_hbm, value_hbm, out_hbm, cot_hbm, turn_hbm) = refs[:10]
    mixed, grad_out = refs[10:12]
    (
        x_rows, conv_w, query_w, key_w, value_w, out_w, cot, turn, fetched,
        edges, edge_sems, spread, stacked, pooled, normed, queries, kv, values, kv_sems, bias, gain,
    ) = refs[12:33]
    gradient_refs = refs[33:]
    cot_t, att = gradient_refs[:2]
    tokens, rows = plan.tokens, 2 * plan.tokens
    s = lax.axis_index("seq")
    last = plan.seq - 1
    tiles = plan.width // TILE
    taps, channels = KERNEL_TAPS, x_rows.shape[1]

    def conv_fetch(n):
        return pltpu.make_async_copy(
            conv_hbm.at[:, pl.ds(pl.multiple_of(n * TILE, TILE), TILE)],
            conv_w.at[n],
            fetched.at[8 + n],
        )

    x_fetch = pltpu.make_async_copy(x_hbm, x_rows, fetched.at[0])
    key_fetch = pltpu.make_async_copy(key_hbm, key_w, fetched.at[1])
    value_fetch = pltpu.make_async_copy(value_hbm, value_w, fetched.at[2])
    turn_fetch = pltpu.make_async_copy(
        turn_hbm.at[pl.ds(pl.multiple_of(s * tokens, tokens), tokens)], turn, fetched.at[3]
    )
    query_fetch = pltpu.make_async_copy(query_hbm, query_w, fetched.at[4])
    cot_fetch = pltpu.make_async_copy(cot_hbm, cot, fetched.at[5])
    out_fetch = pltpu.make_async_copy(out_hbm, out_w, fetched.at[6])
    x_fetch.start()
    for n in range(tiles):
        conv_fetch(n).start()
    for fetch in (key_fetch, value_fetch, turn_fetch, query_fetch, cot_fetch, out_fetch):
        fetch.start()

    bias[...] = bias_in[...].reshape(bias.shape)
    gain[...] = gain_in[...].reshape(gain.shape)
    greet(plan)

    def edge_ahead():
        return remote(
            x_hbm.at[pl.ds(rows - EDGE, EDGE)], edges.at[0], edge_sems.at[0], edge_sems.at[1],
            {"seq": s + 1},
        )

    def edge_back():
        return remote(
            x_hbm.at[pl.ds(0, EDGE)], edges.at[1], edge_sems.at[2], edge_sems.at[3],
            {"seq": s - 1},
        )

    blocks = channels // 128
    if last > 0:

        @pl.when(s < last)
        def _():
            edge_ahead().start()

        @pl.when(s > 0)
        def _():
            edge_back().start()

    x_fetch.wait()
    for j in range(blocks):
        spread[j, EDGE : EDGE + rows, :] = x_rows[:, j * 128 : (j + 1) * 128].astype(jnp.float32)
    blank = jnp.zeros((EDGE, 128), jnp.float32)
    for j in range(blocks):
        spread[j, :EDGE, :] = blank
        spread[j, EDGE + rows :, :] = blank

    def stack(tap, first, count):
        for parity in range(2):
            for j in range(blocks):
                start = EDGE + parity + DILATION_STEP * (tap - 1) + 2 * first
                lane = tap * channels + j * 128
                row = parity * tokens + first
                stacked[row : row + count, lane : lane + 128] = spread[
                    j, pl.ds(start, count, stride=2), :
                ].astype(jnp.bfloat16)

    for tap in range(taps):
        stack(tap, 0, tokens)

    def put_edge(which, start, tap, first):
        (edge_ahead if which == 0 else edge_back)().wait_recv()
        for j in range(blocks):
            spread[j, start : start + EDGE, :] = edges[which, :, j * 128 : (j + 1) * 128].astype(
                jnp.float32
            )
        stack(tap, first, EDGE)

    if last > 0:

        @pl.when(s > 0)
        def _():
            put_edge(0, 0, 0, 0)

        @pl.when(s < last)
        def _():
            put_edge(1, EDGE + rows, taps - 1, tokens - EDGE)

    def conv_tile(n, carry):
        conv_fetch(n).wait()
        columns = pl.ds(pl.multiple_of(n * TILE, TILE), TILE)
        pre = (
            jnp.dot(stacked[...], conv_w[n], preferred_element_type=jnp.float32)
            + bias[:, columns]
        )
        inner = math.sqrt(2.0 / math.pi) * (pre + 0.044715 * (pre * pre * pre))
        activated = pre * (0.5 * (1.0 + jnp.tanh(inner)))
        pooled[:, columns] = jnp.maximum(activated[:tokens], activated[tokens:]).astype(
            jnp.bfloat16
        )
        return carry

    lax.fori_loop(0, tiles, conv_tile, 0)

    part = 32

    def norm_part(i, carry):
        here = pl.ds(pl.multiple_of(i * part, part), part)
        wide = pooled[here, :].astype(jnp.float32)
        squares = jnp.mean(wide * wide, axis=-1, keepdims=True)
        normed[here, :] = (wide * lax.rsqrt(squares + norm_eps) * gain[...]).astype(jnp.bfloat16)
        return carry

    lax.fori_loop(0, tokens // part, norm_part, 0)

    key_fetch.wait()
    value_fetch.wait()
    turn_fetch.wait()

    def turned(vectors):
        return (
            vectors * turn[:, :KEY] + pltpu.roll(vectors, KEY // 2, 1) * turn[:, KEY:]
        ).astype(jnp.bfloat16)

    half = tokens // 2
    kv[s, :tokens, :] = turned(
        jnp.dot(normed[...], key_w[...], preferred_element_type=jnp.float32)
    )
    own_values = lax.dot_general(
        normed[...], value_w[...], (((1,), (1,)), ((), ())), preferred_element_type=jnp.float32
    )
    kv[s, tokens : 2 * tokens, :] = own_values[:, :128].astype(jnp.bfloat16)
    kv[s, 2 * tokens :, :] = jnp.concatenate(
        [own_values[:half, 128:], own_values[half:, 128:]], axis=1
    ).astype(jnp.bfloat16)
    split = 5 * tokens // 4

    def kv_copy(way, hop, h):
        owner = s - hop if way == 0 else s + hop
        owner = jnp.clip(owner, 0, last)
        at = ((way * last + hop) * 2 + h) * 2
        block = kv.at[owner, pl.ds(h * split, split)]
        return remote(
            block, block, kv_sems.at[at], kv_sems.at[at + 1],
            {"seq": s + 1 if way == 0 else s - 1},
        )

    def kv_sent(way, hop):
        if way == 0:
            return jnp.logical_and(s >= hop, s < last)
        return jnp.logical_and(s + hop <= last, s > 0)

    for way in range(2) if last > 0 else ():

        @pl.when(kv_sent(way, 0))
        def _(way=way):
            kv_copy(way, 0, 0).start()
            kv_copy(way, 0, 1).start()

    query_fetch.wait()

    def query_pair(c, carry):
        pair = jnp.dot(
            normed[...],
            query_w[:, pl.ds(pl.multiple_of(c * 2 * KEY, 2 * KEY), 2 * KEY)],
            preferred_element_type=jnp.float32,
        )
        queries[2 * c] = turned(pair[:, :KEY])
        queries[2 * c + 1] = turned(pair[:, KEY:])
        return carry

    lax.fori_loop(0, plan.chunks, query_pair, 0)
    cot_fetch.wait()
    turn_over(plan, cot, cot_t)
    out_fetch.wait()
    for hop in range(last):
        for h in range(2):
            for way in range(2):
                got = s > hop if way == 0 else s + hop < last

                @pl.when(got)
                def _(hop=hop, h=h, way=way):
                    kv_copy(way, hop, h).wait_recv()

                    @pl.when(s < last if way == 0 else s > 0)
                    def _():
                        if hop + 1 < last:
                            kv_copy(way, hop + 1, h).start()

    for j in range(plan.seq):
        values[j, :, :128] = kv[j, tokens : 2 * tokens, :]
        values[j, :half, 128:] = kv[j, 2 * tokens :, : VAL - 128]
        values[j, half:, 128:] = kv[j, 2 * tokens :, VAL - 128 :]

    def attend_head(h):
        scores = lax.dot_general(
            queries[h],
            kv[:, :tokens, :].reshape(plan.seq * tokens, KEY),
            (((1,), (1,)), ((), ())),
            preferred_element_type=jnp.float32,
        )
        peak = jnp.max(scores, axis=-1, keepdims=True)
        weights = jnp.exp2((scores - peak) * (KEY ** (-0.5) * math.log2(math.e)))
        total = jnp.sum(weights, axis=-1, keepdims=True)
        weighted = jnp.dot(
            weights.astype(jnp.bfloat16),
            values[...].reshape(plan.seq * tokens, VAL),
            preferred_element_type=jnp.float32,
        )
        return weighted / total

    def produce(t):
        @pl.when(jnp.logical_and(t < plan.units, t % plan.pieces == 0))
        def _():
            c = t // plan.pieces
            att[c] = jnp.concatenate([attend_head(2 * c), attend_head(2 * c + 1)], axis=1).astype(
                jnp.bfloat16
            )

        @pl.when(jnp.logical_and(t >= plan.units, t < plan.units + tiles))
        def _():
            columns = pl.ds(pl.multiple_of((t - plan.units) * TILE, TILE), TILE)
            total = pooled[:, columns].astype(jnp.float32)
            for c in range(plan.chunks):
                total = total + jnp.dot(
                    att[c],
                    out_w[c * plan.chunk : (c + 1) * plan.chunk, columns],
                    preferred_element_type=jnp.float32,
                )
            mixed[:, columns] = total.astype(jnp.bfloat16)

    gradient_loop(plan, gradient_refs, grad_out, produce, plan.units + tiles)

    for hop in range(last):
        for way in range(2):

            @pl.when(kv_sent(way, hop))
            def _(hop=hop, way=way):
                kv_copy(way, hop, 0).wait_send()
                kv_copy(way, hop, 1).wait_send()

    if last > 0:

        @pl.when(s < last)
        def _():
            edge_ahead().wait_send()

        @pl.when(s > 0)
        def _():
            edge_back().wait_send()


def turn_table(count):
    frequency = np.exp(
        np.float32(-math.log(rope_base) * 2.0) * np.arange(KEY // 2, dtype=np.float32) / KEY
    ).astype(np.float32)
    angles = np.arange(count, dtype=np.float32)[:, None] * frequency[None, :]
    cosine, sines = np.cos(angles), np.sin(angles)
    return np.concatenate([cosine, cosine, -sines, sines], axis=1).astype(np.float32)


def section(x_in, kernel_weight, conv_bias, norm_gain, w_query, w_key, w_value, w_out, cotangent):
    inputs, upstream = x_in[0], cotangent[0]
    rows, channels = inputs.shape
    width = kernel_weight.shape[2]
    plan = Plan(
        rows // 2, width, w_out.shape[0], lax.axis_size("dp"), lax.axis_size("seq")
    )
    tokens, seq, tiles = plan.tokens, plan.seq, width // TILE
    depth = KERNEL_TAPS * channels
    bf = jnp.bfloat16
    held = pl.BlockSpec(memory_space=pltpu.VMEM)
    away = pl.BlockSpec(memory_space=pl.ANY)
    mixed, gradient = pl.pallas_call(
        functools.partial(section_kernel, plan),
        out_shape=(
            jax.ShapeDtypeStruct((tokens, width), bf),
            jax.ShapeDtypeStruct((plan.block, plan.columns), bf),
        ),
        in_specs=[away, away, held, held, away, away, away, away, away, away],
        out_specs=(held, held),
        scratch_shapes=[
            pltpu.VMEM((rows, channels), bf),
            pltpu.VMEM((tiles, depth, TILE), bf),
            pltpu.VMEM(w_query.shape, bf),
            pltpu.VMEM(w_key.shape, bf),
            pltpu.VMEM(w_value.shape[::-1], bf),
            pltpu.VMEM(w_out.shape, bf),
            pltpu.VMEM((tokens, width), bf),
            pltpu.VMEM((tokens, 2 * KEY), jnp.float32),
            pltpu.SemaphoreType.DMA((8 + tiles,)),
            pltpu.VMEM((2, EDGE, channels), bf),
            pltpu.SemaphoreType.DMA((4,)),
            pltpu.VMEM((channels // 128, rows + 2 * EDGE, 128), jnp.float32),
            pltpu.VMEM((rows, depth), bf),
            pltpu.VMEM((tokens, width), bf),
            pltpu.VMEM((tokens, width), bf),
            pltpu.VMEM((w_query.shape[1] // KEY, tokens, KEY), bf),
            pltpu.VMEM((seq, 5 * tokens // 2, KEY), bf),
            pltpu.VMEM((seq, tokens, VAL), bf),
            pltpu.SemaphoreType.DMA((8 * max(seq - 1, 1),)),
            pltpu.VMEM((1, width), jnp.float32),
            pltpu.VMEM((1, width), jnp.float32),
        ]
        + plan.scratch(),
        compiler_params=pltpu.CompilerParams(
            collective_id=1, has_side_effects=True, vmem_limit_bytes=60 * 2**20
        ),
        name="section",
    )(
        inputs,
        kernel_weight.reshape(depth, width),
        conv_bias,
        norm_gain,
        w_query,
        w_key,
        jnp.transpose(w_value),
        w_out,
        upstream,
        turn_table(tokens * seq),
    )
    return mixed[None], gradient.astype(jnp.float32)


def local(x_in, kernel_weight, conv_bias, norm_gain, w_query, w_key, w_value, w_out, cotangent):
    inputs = x_in[0]
    edge_padding = DILATION_STEP * (KERNEL_TAPS - 1) // 2
    padded_rows = padded(inputs, (("seq", 0),), edge_padding)
    padded_row_count = inputs.shape[0]
    before_activation = jnp.broadcast_to(
        conv_bias[None, :], (padded_row_count, kernel_weight.shape[2])
    )
    for kernel_tap_index in range(KERNEL_TAPS):
        before_activation = before_activation + jnp.dot(
            padded_rows[
                kernel_tap_index * DILATION_STEP : kernel_tap_index * DILATION_STEP
                + padded_row_count
            ],
            kernel_weight[kernel_tap_index],
            preferred_element_type=jnp.float32,
        )
    activated = jax.nn.gelu(before_activation)
    pooled = jnp.max(activated.reshape(padded_row_count // 2, 2, -1), axis=1).astype(jnp.bfloat16)
    token_count = pooled.shape[0]
    features = lax.all_gather(pooled, "head", axis=1, tiled=True)
    widened = features.astype(jnp.float32)
    squares = jnp.mean(widened * widened, axis=-1, keepdims=True)
    normed = (widened * lax.rsqrt(squares + norm_eps) * norm_gain).astype(jnp.bfloat16)
    seq_offset = lax.axis_index("seq") * token_count
    positions = seq_offset + jnp.arange(token_count, dtype=jnp.int32)
    local_heads = w_query.shape[1] // KEY
    queries = rotate(
        jnp.dot(normed, w_query, preferred_element_type=jnp.float32).reshape(
            token_count, local_heads, KEY
        ),
        positions,
    ).astype(jnp.bfloat16)
    own_rows = token_count // lax.axis_size("head")
    row_offset = lax.axis_index("head") * own_rows
    own_normed = lax.dynamic_slice_in_dim(normed, row_offset, own_rows, 0)
    own_positions = seq_offset + row_offset + jnp.arange(own_rows, dtype=jnp.int32)
    key_rows = rotate(
        jnp.dot(own_normed, w_key, preferred_element_type=jnp.float32), own_positions
    ).astype(jnp.bfloat16)
    value_rows = jnp.dot(own_normed, w_value, preferred_element_type=jnp.float32).astype(
        jnp.bfloat16
    )
    start_state = (
        jnp.full((local_heads, token_count), -1e30, jnp.float32),
        jnp.zeros((local_heads, token_count), jnp.float32),
        jnp.zeros((token_count, local_heads, VAL), jnp.float32),
    )
    both = lax.all_gather(
        jnp.concatenate([key_rows, value_rows], axis=1), ("seq", "head"), axis=0, tiled=True
    )
    final_state = attend_pieces(
        queries,
        both[:, :KEY],
        both[:, KEY:],
        start_state,
    )
    running_max, running_sum, weighted = final_state
    attended = (
        (weighted / jnp.transpose(running_sum)[:, :, None])
        .astype(jnp.bfloat16)
        .reshape(token_count, local_heads * VAL)
    )
    projected = lax.psum_scatter(
        lax.dot_general(
            w_out, attended, (((0,), (1,)), ((), ())), preferred_element_type=jnp.float32
        ).astype(jnp.bfloat16),
        "head",
        scatter_dimension=0,
        tiled=True,
    ).astype(jnp.float32)
    mixed = (pooled.astype(jnp.float32) + jnp.transpose(projected)).astype(jnp.bfloat16)[None]
    upstream = cotangent[0]
    gradient = reduced_gradient(upstream, attended)
    return (mixed, gradient)


def solution(mesh):
    return jax.shard_map(
        section if mesh.shape["head"] == 1 else local,
        mesh=mesh,
        in_specs=(
            P(("groups", "dp"), "seq", None),
            P(None, None, "head"),
            P("head"),
            P(),
            P(None, "head"),
            P(),
            P(),
            P("head", None),
            P(("groups", "dp"), "seq", None),
        ),
        out_specs=(P(("groups", "dp"), "seq", "head"), P(("groups", "dp"), "head")),
        check_vma=False,
    )
```
